32 devices in a mesh: grp: 2 (over y), tm: 4 (over z), space: 2 (over x), obs: 2 (over core).
Axes of the slice: x: 2, y: 2, z: 4, core: 2. Of those that a mesh axis runs over, the one named last changes fastest.
Arguments:
- obs_panel: bfloat16 [8192, 768], P(('grp', 'tm', 'space', 'obs')), parts along dimension 0, may hold values from -0.375 to 0.375
- node_index: int32 [8192], P(('grp', 'tm', 'space', 'obs')), parts along dimension 0, may hold values from 0 to 767
- weight: bfloat16 [8192], P(('grp', 'tm', 'space', 'obs')), parts along dimension 0, may hold values from 0.049804688 to 0.5
- residual: bfloat16 [8192], P(('grp', 'tm', 'space', 'obs')), parts along dimension 0, may hold values from -6 to 6
- route_time: int32 [8192], P(('grp', 'tm', 'space', 'obs')), parts along dimension 0, may hold values from 0 to 3, as said below
- spatial_prec: float32 [8, 768, 768], P(('grp', 'tm'), ('space', 'obs')), parts along dimension 0, as said below
- ar_coef: float32 [8], P(('grp', 'tm')), parts along dimension 0, may hold values from 0.5 to 0.85
- prior_rhs: float32 [8, 768], P(('grp', 'tm'), ('space', 'obs')), parts along dimension 0, may hold values from -6 to 6
Outputs:
- reduced_diag: float32 [8, 768, 768], P(('grp', 'tm'), ('space', 'obs')), parts along dimension 0
- fill_block: float32 [8, 768, 768], P(('grp', 'tm'), ('space', 'obs')), parts along dimension 0
- reduced_rhs: float32 [8, 768], P(('grp', 'tm'), ('space', 'obs')), parts along dimension 0
The draws below stay inside these ranges and needn't reach their ends.
There are 2 independent parts, one for each index of `grp`. The reference program is written for one: setup_inputs(seed, part) draws one part's arguments, and reference() takes and returns one part's arrays. A program takes and returns all parts, laid end to end along the dimension named above; each array names one. Nothing has to cross between parts.
Inputs may be any that keep to these rules, and one draw needn't show every extreme that they name: `route_time`: each device's 256 rows name each time block at most 128 times; in every draw one time block receives exactly 128 rows from every device's block of rows. `spatial_prec`: each block is symmetric positive definite.
All inputs are finite; a program needn't handle non-finite values.
Results may differ from the reference program's by a relative error of at most 0.0044.
Values may be sent and summed in bfloat16 or wider, within the bound.
No kernel may reach another device: no remote copies, remote signals or barrier semaphores. Data moves between devices by JAX's collectives and lax.ppermute only.
A program may use at most 64 MiB of HBM per device.

```python
import math
import jax
import jax.numpy as jnp
from jax import lax

B = 768
ROWS_DEV = 256
NT = 4
SOURCES = 16
ROWS_ALL = 4096
ROWS_TIME = 1024
CAP = 128


def draw_route_time(key, part):
    full_time = jax.random.randint(jax.random.fold_in(key, 201), (), 0, NT).astype(jnp.int32)
    others_count = ROWS_DEV - CAP

    def one_source(source_index):
        source_key = jax.random.fold_in(key, source_index + 300)
        slot_picks = jax.random.permutation(jax.random.fold_in(source_key, 1), (NT - 1) * CAP)[:others_count]
        other_time = (slot_picks // CAP).astype(jnp.int32)
        other_time = other_time + (other_time >= full_time).astype(jnp.int32)
        row_times = jnp.concatenate([jnp.full((CAP,), full_time, jnp.int32), other_time])
        shuffle = jax.random.permutation(jax.random.fold_in(source_key, 2), ROWS_DEV)
        return row_times[shuffle]
    return jax.vmap(one_source)(jnp.arange(SOURCES, dtype=jnp.int32)).reshape(ROWS_ALL)


def draw_spatial_prec(key, part):
    mixing_key = jax.random.fold_in(key, 101)
    base_key = jax.random.fold_in(key, 102)
    mixing = jax.random.normal(mixing_key, (NT, B, B), jnp.float32)
    base_diag = jax.random.uniform(base_key, (NT, B), jnp.float32, 1.0, 3.0)
    product = jnp.einsum('tik,tjk->tij', mixing, mixing, precision=lax.Precision.HIGHEST) / B
    symmetric = 0.5 * (product + jnp.swapaxes(product, 1, 2))
    identity = jnp.eye(B, dtype=jnp.float32)
    return symmetric + base_diag[:, :, None] * identity


def plant(result, own_key, smallest, largest):
    longest = result.shape.index(max(result.shape))
    spots = []
    for shift in (0, 1):
        where = [jax.random.randint(jax.random.fold_in(own_key, axis), (), 0, length) for axis, length in enumerate(result.shape)]
        where[longest] = (where[longest] + shift) % result.shape[longest]
        spots.append(tuple(where))
    return result.at[spots[0]].set(smallest).at[spots[1]].set(largest)


def steps_of(own_key, shape, shards, smallest, largest):
    def one(axis_at, blocks):
        draws = jax.random.uniform(jax.random.fold_in(jax.random.fold_in(own_key, 6), axis_at), (blocks,), jnp.float32, smallest / len(shards), largest / len(shards))
        return jnp.repeat(jnp.exp(draws), shape[axis_at] // blocks).reshape((-1,) + (1,) * (len(shape) - axis_at - 1))

    level = one(*shards[0])
    for cut in shards[1:]:
        level = level * one(*cut)
    return level


def noise(stream_key, shape, spread, limit, cuts=(), kind=jnp.bfloat16):
    level = steps_of(stream_key, shape, cuts, -0.22, 0.18) if cuts else 1.0
    entries = jax.random.normal(stream_key, shape, jnp.float32) * spread * level
    return jnp.minimum(jnp.maximum(entries, -limit), limit).astype(kind)


def setup_inputs(seed: int = 0, part: int = 0) -> dict:
    arg_keys = jax.random.split(jax.random.key(seed), 9)
    part_splits = jax.random.split(jax.random.fold_in(arg_keys[8], part), 9)
    obs_panel = noise(part_splits[0], (ROWS_ALL, B), (ROWS_TIME // 4) ** -0.5, 0.375, ((0, 16),))
    node_index = plant(jax.random.randint(part_splits[1], (ROWS_ALL,), 0, B), jax.random.fold_in(part_splits[1], 1), 0, B - 1).astype(jnp.int32)
    weight = jnp.clip(jnp.exp(math.log(0.5) - 2.306499 * jax.random.uniform(part_splits[2], (ROWS_ALL,), jnp.float32) ** steps_of(part_splits[2], (ROWS_ALL,), ((0, 16),), -0.2, 0.2)), 0.049804688, 0.5).astype(jnp.bfloat16)
    residual = noise(part_splits[3], (ROWS_ALL,), 1.0, 6.0, ((0, 16),))
    route_time = draw_route_time(jax.random.fold_in(jax.random.fold_in(arg_keys[8], part), 71), part)
    spatial_prec = draw_spatial_prec(jax.random.fold_in(jax.random.fold_in(arg_keys[8], part), 71), part)
    ar_coef = jnp.clip(0.5 + 0.35000002 * jax.random.uniform(part_splits[6], (NT,), jnp.float32) ** steps_of(part_splits[6], (NT,), ((0, 4),), -0.2, 0.2), 0.5, 0.85)
    prior_rhs = noise(part_splits[7], (NT, B), 1.0, 6.0, ((0, 4), (1, 4)), jnp.float32)
    return dict(obs_panel=obs_panel, node_index=node_index, weight=weight, residual=residual, route_time=route_time, spatial_prec=spatial_prec, ar_coef=ar_coef, prior_rhs=prior_rhs)


HIGHEST = lax.Precision.HIGHEST

def eliminate(diag_block, rhs_vec, left_couple, right_couple):
    count = diag_block.shape[0]
    factor = jnp.linalg.cholesky(diag_block)
    stacked = jnp.concatenate([left_couple.T, right_couple, rhs_vec[:, None]], axis=1)
    solved = lax.linalg.triangular_solve(factor, stacked, left_side=True, lower=True)
    left_y = solved[:, :count]
    right_y = solved[:, count:2 * count]
    reduced = solved[:, 2 * count]
    left_b = left_y.astype(jnp.bfloat16)
    right_b = right_y.astype(jnp.bfloat16)
    loss_left = jnp.dot(left_b.T.astype(jnp.float32), left_b.astype(jnp.float32), preferred_element_type=jnp.float32)
    loss_right = jnp.dot(right_b.T.astype(jnp.float32), right_b.astype(jnp.float32), preferred_element_type=jnp.float32)
    fill_new = -jnp.dot(left_b.T.astype(jnp.float32), right_b.astype(jnp.float32), preferred_element_type=jnp.float32)
    up_left = jnp.dot(reduced, left_y, precision=HIGHEST)
    up_right = jnp.dot(reduced, right_y, precision=HIGHEST)
    return (loss_left, loss_right, fill_new, up_left, up_right)

def reference(obs_panel, node_index, weight, residual, route_time, spatial_prec, ar_coef, prior_rhs):
    weighted_res = (weight.astype(jnp.float32) * residual.astype(jnp.float32)).astype(jnp.bfloat16)
    node_hits = (node_index[:, None] == jnp.arange(B, dtype=jnp.int32)[None, :]).astype(jnp.float32)
    design = (obs_panel.astype(jnp.float32) + node_hits).astype(jnp.bfloat16)
    weighted = (weight.astype(jnp.float32)[:, None] * design.astype(jnp.float32)).astype(jnp.bfloat16)
    row_order = jnp.argsort(route_time, stable=True).astype(jnp.int32)
    counts = jnp.sum((route_time[:, None] == jnp.arange(NT, dtype=jnp.int32)[None, :]).astype(jnp.int32), axis=0)
    starts = (jnp.cumsum(counts) - counts).astype(jnp.int32)
    most_rows = SOURCES * CAP
    padding = jnp.zeros((most_rows, B), jnp.bfloat16)
    sorted_design = jnp.concatenate([design[row_order], padding], axis=0)
    sorted_weighted = jnp.concatenate([weighted[row_order], padding], axis=0)
    sorted_res = jnp.concatenate([weighted_res[row_order], jnp.zeros((most_rows,), jnp.bfloat16)], axis=0)

    def per_time(time_step):
        begin = starts[time_step]
        live_rows = (jnp.arange(most_rows, dtype=jnp.int32) < counts[time_step]).astype(jnp.float32)
        rows_design = lax.dynamic_slice_in_dim(sorted_design, begin, most_rows, 0).astype(jnp.float32)
        rows_weighted = lax.dynamic_slice_in_dim(sorted_weighted, begin, most_rows, 0).astype(jnp.float32) * live_rows[:, None]
        rows_res = lax.dynamic_slice_in_dim(sorted_res, begin, most_rows, 0).astype(jnp.float32) * live_rows
        gram_part = jnp.dot(rows_design.T, rows_weighted, precision=HIGHEST)
        grad_part = jnp.dot(rows_res, rows_design, precision=HIGHEST)
        return (gram_part, grad_part)
    grams, grads = lax.map(per_time, jnp.arange(NT, dtype=jnp.int32))
    next_prec = jnp.roll(spatial_prec, -1, axis=0)
    next_coef = jnp.roll(ar_coef, -1)
    diag_one = spatial_prec + (next_coef * next_coef)[:, None, None] * next_prec + grams
    rhs_one = prior_rhs + grads
    couple = -next_coef[:, None, None] * next_prec
    diag_two = [diag_one[step] for step in range(NT)]
    rhs_two = [rhs_one[step] for step in range(NT)]
    fills_one = {}
    for time_step in range(1, NT, 2):
        left_time = time_step - 1
        right_time = (time_step + 1) % NT
        loss_left, loss_right, fill_new, up_left, up_right = eliminate(diag_one[time_step], rhs_one[time_step], couple[left_time], couple[time_step])
        diag_two[left_time] = diag_two[left_time] - loss_left
        diag_two[right_time] = diag_two[right_time] - loss_right
        rhs_two[left_time] = rhs_two[left_time] - up_left
        rhs_two[right_time] = rhs_two[right_time] - up_right
        fills_one[time_step] = fill_new
    diag_three = list(diag_two)
    rhs_three = list(rhs_two)
    fills_two = {}
    for time_step in range(2, NT, 4):
        left_time = time_step - 2
        right_time = (time_step + 2) % NT
        loss_left, loss_right, fill_new, up_left, up_right = eliminate(diag_two[time_step], rhs_two[time_step], fills_one[time_step - 1], fills_one[time_step + 1])
        diag_three[left_time] = diag_three[left_time] - loss_left
        diag_three[right_time] = diag_three[right_time] - loss_right
        rhs_three[left_time] = rhs_three[left_time] - up_left
        rhs_three[right_time] = rhs_three[right_time] - up_right
        fills_two[time_step] = fill_new
    fill_list = []
    for time_step in range(NT):
        if time_step % 2 == 1:
            fill_list.append(fills_one[time_step])
        elif time_step % 4 == 2:
            fill_list.append(fills_two[time_step])
        else:
            fill_list.append(jnp.zeros((B, B), jnp.float32))
    return (jnp.stack(diag_three), jnp.stack(fill_list), jnp.stack(rhs_three))
```

```python
import jax
import jax.numpy as jnp
from jax import lax
from jax.experimental import pallas as pl
from jax.experimental.pallas import tpu as pltpu
from jax.sharding import PartitionSpec as P


def from_behind(value, axis, steps):
    count = lax.axis_size(axis)
    pairs = [(source, (source + steps) % count) for source in range(count)]
    return lax.ppermute(value, axis, pairs)


def slot_table(route_time, n_times, capacity):
    marks = (route_time[:, None] == lax.iota(jnp.int32, n_times)[None, :]).astype(jnp.int32)
    before = jnp.cumsum(marks, axis=0) - marks
    rank = jnp.sum(before * marks, axis=1)
    return route_time * capacity + rank


def to_time(payload, shift_by):
    return from_behind(payload, "tm", shift_by)


BLOCK = 128
PANEL = 8
HIGHEST = lax.Precision.HIGHEST


def across(value, lane_index):
    return jnp.broadcast_to(value[:, lane_index : lane_index + 1], value.shape)


def down(value, row_index):
    return jnp.broadcast_to(value[row_index : row_index + 1, :], value.shape)


def tree_sum(terms):
    terms = list(terms)
    while len(terms) > 1:
        terms = [
            terms[at] + terms[at + 1] if at + 1 < len(terms) else terms[at]
            for at in range(0, len(terms), 2)
        ]
    return terms[0]


def dot32(left, right, dims=((1,), (0,))):
    return lax.dot_general(
        left, right, (dims, ((), ())), precision=HIGHEST, preferred_element_type=jnp.float32
    )


def halves(value):
    high = value.astype(jnp.bfloat16)
    return high, (value - high.astype(jnp.float32)).astype(jnp.bfloat16)


def dot_halves(left, right, dims=((1,), (0,))):
    def one(a, b):
        return lax.dot_general(a, b, (dims, ((), ())), preferred_element_type=jnp.float32)

    return one(left[0], right[0]) + (one(left[0], right[1]) + one(left[1], right[0]))


def panel_step(panel, first, lane, sub, ones):
    cols = [across(panel, first + j) * ones for j in range(PANEL)]
    entry = [[None] * PANEL for _ in range(PANEL)]
    for i in range(PANEL):
        for j in range(i, PANEL):
            entry[i][j] = entry[j][i] = down(cols[j], i)
    inside = (lane >= first) & (lane < first + PANEL)
    augmented = jnp.where(inside, jnp.where(lane == first + sub, 1.0, 0.0), panel)
    lower = jnp.where(lane < first + PANEL, augmented, 0.0)
    rows = [down(augmented, i) for i in range(PANEL)]
    for j in range(0, PANEL, 2):
        p, b, s = entry[j][j], entry[j][j + 1], entry[j + 1][j + 1]
        r = 1.0 / (p * s - b * b)
        upper_new, lower_new = {}, {}
        for m in range(j + 2, PANEL):
            upper_new[m] = (s * entry[j][m] - b * entry[j + 1][m]) * r
            lower_new[m] = (p * entry[j + 1][m] - b * entry[j][m]) * r
        upper_row = (s * rows[j] - b * rows[j + 1]) * r
        lower_row = (p * rows[j + 1] - b * rows[j]) * r
        for i in range(PANEL):
            if i in (j, j + 1):
                continue
            f, g = entry[i][j], entry[i][j + 1]
            for m in range(max(j + 2, i if i > j else 0), PANEL):
                value = entry[i][m] - (f * upper_new[m] + g * lower_new[m])
                entry[i][m] = value
                if i > j and m > i:
                    entry[m][i] = value
            rows[i] = rows[i] - (f * upper_row + g * lower_row)
        for m in range(j + 2, PANEL):
            entry[j][m] = upper_new[m]
            entry[j + 1][m] = lower_new[m]
        rows[j], rows[j + 1] = upper_row, lower_row
    solved = rows[0]
    for i in range(1, PANEL):
        solved = jnp.where(sub == i, rows[i], solved)
    return lower, rows, solved, inside


def factor_block(block, lower_ref, scaled_ref, ones):
    count = BLOCK // PANEL
    lane = lax.broadcasted_iota(jnp.int32, (PANEL, BLOCK), 1)
    sub = lax.broadcasted_iota(jnp.int32, (PANEL, BLOCK), 0)
    rows = [block[PANEL * i : PANEL * (i + 1), :] for i in range(count)]
    for q in range(count):
        first = q * PANEL
        lower, pivot_rows, solved, inside = panel_step(rows[q], first, lane, sub, ones)
        lower_ref[first : first + PANEL, :] = lower
        scaled_ref[first : first + PANEL, :] = jnp.where(lane < first + PANEL, solved, 0.0)
        for i in range(q + 1, count):
            change = tree_sum(
                across(rows[i], first + j) * pivot_rows[j] for j in range(PANEL)
            )
            rows[i] = jnp.where(inside, 0.0, rows[i]) - change


def solve_kernel(diag_ref, cols_ref, out_ref, work_ref, lower_ref, scaled_ref, ones_ref):
    blocks = diag_ref.shape[0] // BLOCK
    ones_ref[...] = jnp.ones_like(ones_ref)
    ones = ones_ref[...]
    work_ref[...] = diag_ref[...]
    out_ref[...] = cols_ref[...]
    current = diag_ref[0:BLOCK, 0:BLOCK]
    for p in range(blocks):
        at, after = p * BLOCK, (p + 1) * BLOCK
        last = p == blocks - 1
        slot = p % 2
        factor_block(current, lower_ref.at[slot], scaled_ref.at[slot], ones)
        lower, scaled = lower_ref[slot], scaled_ref[slot]
        if not last:
            below = dot32(work_ref[after : after + BLOCK, at:after], lower, ((1,), (1,)))
            beside = dot32(scaled, work_ref[at:after, after : after + BLOCK])
            current = work_ref[after : after + BLOCK, after : after + BLOCK] - dot32(below, beside)
        inverse = halves(dot32(lower, scaled, ((0,), (0,))))
        if not last:
            panel = dot_halves(inverse, halves(work_ref[at:after, after:]))
            panel_parts = halves(panel)
        panel_cols = dot_halves(inverse, halves(out_ref[at:after, :]))
        panel_cols_parts = halves(panel_cols)
        for i in range(blocks):
            if i == p:
                continue
            rows = slice(i * BLOCK, (i + 1) * BLOCK)
            column = halves(work_ref[rows, at:after])
            if not last:
                work_ref[rows, after:] -= dot_halves(column, panel_parts)
            out_ref[rows, :] -= dot_halves(column, panel_cols_parts)
        if not last:
            work_ref[at:after, after:] = panel
        out_ref[at:after, :] = panel_cols


def solve(diag, cols):
    nodes, width = cols.shape
    assert nodes % BLOCK == 0, nodes
    whole = pl.BlockSpec(memory_space=pltpu.VMEM)
    return pl.pallas_call(
        solve_kernel,
        out_shape=jax.ShapeDtypeStruct((nodes, width), jnp.float32),
        in_specs=[whole, whole],
        out_specs=whole,
        scratch_shapes=[
            pltpu.VMEM((nodes, nodes), jnp.float32),
            pltpu.VMEM((2, BLOCK, BLOCK), jnp.float32),
            pltpu.VMEM((2, BLOCK, BLOCK), jnp.float32),
            pltpu.VMEM((PANEL, BLOCK), jnp.float32),
        ],
        cost_estimate=pl.CostEstimate(
            flops=40 * nodes * nodes * nodes, bytes_accessed=4 * nodes * nodes, transcendentals=0
        ),
        name="solve_spd",
    )(diag, cols)


def product(columns, full_rows):
    high, low = halves(columns)

    def one(part):
        return lax.dot_general(
            part, full_rows, (((0,), (1,)), ((), ())), preferred_element_type=jnp.float32
        )

    return one(high) + one(low)


def eliminate(diag_rows, rhs_rows, left_cols, right_cols, with_turn):
    shard_rows = diag_rows.shape[0]
    full_diag, full_rhs = (
        lax.all_gather(diag_rows, ("space", "obs"), axis=0, tiled=True),
        lax.all_gather(rhs_rows, ("space", "obs"), axis=0, tiled=True),
    )
    left_full, right_full = lax.all_gather(
        (left_cols.T.astype(jnp.bfloat16), right_cols.T.astype(jnp.bfloat16)),
        ("space", "obs"),
        axis=0,
        tiled=True,
    )
    solved = solve(full_diag, jnp.concatenate([left_cols, right_cols], axis=1))
    left_x = solved[:, :shard_rows]
    right_x = solved[:, shard_rows:]
    up_left = jnp.dot(full_rhs, left_x, precision=HIGHEST)
    up_right = jnp.dot(full_rhs, right_x, precision=HIGHEST)
    turned = None
    if with_turn:
        turned = -product(right_x, left_full)
    return (
        product(left_x, left_full),
        product(right_x, right_full),
        -product(left_x, right_full),
        turned,
        up_left,
        up_right,
    )


def local(obs_panel, node_index, weight, residual, route_time, spatial_prec, ar_coef, prior_rhs):
    n_times = lax.axis_size("tm")
    time_index = lax.axis_index("tm")
    cell_index = lax.axis_index(("space", "obs"))
    rows_dev, node_count = obs_panel.shape
    shard_rows = spatial_prec.shape[1]
    capacity = 2 * rows_dev // n_times
    slot_count = n_times * capacity
    weighted_res = (weight.astype(jnp.float32) * residual.astype(jnp.float32)).astype(jnp.bfloat16)
    node_hits = (node_index[:, None] == lax.iota(jnp.int32, node_count)[None, :]).astype(
        jnp.float32
    )
    design = (obs_panel.astype(jnp.float32) + node_hits).astype(jnp.bfloat16)
    slot_index = slot_table(route_time, n_times, capacity)
    send_design = jnp.zeros((slot_count, node_count), jnp.bfloat16).at[slot_index].set(design)
    send_weight = jnp.zeros((slot_count,), jnp.bfloat16).at[slot_index].set(weight)
    send_res = jnp.zeros((slot_count,), jnp.bfloat16).at[slot_index].set(weighted_res)
    arrived = (
        lax.all_to_all(
            send_design.reshape(n_times, capacity, node_count),
            "tm",
            split_axis=0,
            concat_axis=0,
            tiled=True,
        ),
        lax.all_to_all(
            send_weight.reshape(n_times, capacity), "tm", split_axis=0, concat_axis=0, tiled=True
        ),
        lax.all_to_all(
            send_res.reshape(n_times, capacity), "tm", split_axis=0, concat_axis=0, tiled=True
        ),
    )
    slot_design = arrived[0].reshape(slot_count, node_count)
    slot_weight = arrived[1].reshape(slot_count)
    slot_res = arrived[2].reshape(slot_count)
    weighted = (slot_weight.astype(jnp.float32)[:, None] * slot_design.astype(jnp.float32)).astype(
        jnp.bfloat16
    )
    grad_part = jnp.dot(slot_res, slot_design, preferred_element_type=jnp.float32)
    gram_part = lax.psum_scatter(
        lax.dot_general(
            slot_design, weighted, (((0,), (0,)), ((), ())), preferred_element_type=jnp.float32
        ),
        ("space", "obs"),
        scatter_dimension=0,
        tiled=True,
    )
    grad_full = lax.psum(grad_part, ("space", "obs"))
    grad_mine = lax.dynamic_slice_in_dim(grad_full, cell_index * shard_rows, shard_rows)
    own_prec = spatial_prec[0]
    own_coef = ar_coef[0]
    next_prec, next_coef_arr = to_time((own_prec, ar_coef), -1)
    next_coef = next_coef_arr[0]
    diag_one = own_prec + next_coef * next_coef * next_prec + gram_part
    rhs_one = prior_rhs[0] + grad_mine
    left_cols = (-own_coef * own_prec).T
    right_cols = (-next_coef * next_prec).T
    loss_left, loss_right, fill_one, turn_one, up_left, up_right = eliminate(
        diag_one, rhs_one, left_cols, right_cols, True
    )
    from_right = to_time((loss_left, up_left, turn_one), -1)
    from_left = to_time((loss_right, up_right, fill_one), 1)
    even_time = time_index % 2 == 0
    diag_two = jnp.where(even_time, diag_one - from_right[0] - from_left[0], diag_one)
    rhs_two = jnp.where(even_time, rhs_one - from_right[1] - from_left[1], rhs_one)
    loss_left2, loss_right2, fill_two, unused_turn, up_left2, up_right2 = eliminate(
        diag_two, rhs_two, from_left[2].T, from_right[2].T, False
    )
    back_right = to_time((loss_left2, up_left2), -2)
    back_left = to_time((loss_right2, up_right2), 2)
    survive = time_index % 4 == 0
    diag_three = jnp.where(survive, diag_two - back_right[0] - back_left[0], diag_two)
    rhs_three = jnp.where(survive, rhs_two - back_right[1] - back_left[1], rhs_two)
    fill_out = jnp.where(
        time_index % 2 == 1,
        fill_one,
        jnp.where(time_index % 4 == 2, fill_two, jnp.zeros_like(fill_two)),
    )
    return (diag_three[None], fill_out[None], rhs_three[None])


def solution(mesh):
    return jax.shard_map(
        local,
        mesh=mesh,
        in_specs=(
            P(("grp", "tm", "space", "obs"), None),
            P(("grp", "tm", "space", "obs")),
            P(("grp", "tm", "space", "obs")),
            P(("grp", "tm", "space", "obs")),
            P(("grp", "tm", "space", "obs")),
            P(("grp", "tm"), ("space", "obs"), None),
            P(("grp", "tm")),
            P(("grp", "tm"), ("space", "obs")),
        ),
        out_specs=(
            P(("grp", "tm"), ("space", "obs"), None),
            P(("grp", "tm"), ("space", "obs"), None),
            P(("grp", "tm"), ("space", "obs")),
        ),
        check_vma=False,
    )
```

```python
import jax
import jax.numpy as jnp
from jax import lax
from jax.experimental import pallas as pl
from jax.experimental.pallas import tpu as pltpu
from jax.sharding import PartitionSpec as P


BLOCK = 128
PANEL = 8
HIGHEST = lax.Precision.HIGHEST


def across(value, lane_index):
    return jnp.broadcast_to(value[:, lane_index : lane_index + 1], value.shape)


def down(value, row_index):
    return jnp.broadcast_to(value[row_index : row_index + 1, :], value.shape)


def tree_sum(terms):
    terms = list(terms)
    while len(terms) > 1:
        terms = [
            terms[at] + terms[at + 1] if at + 1 < len(terms) else terms[at]
            for at in range(0, len(terms), 2)
        ]
    return terms[0]


def dot32(left, right, dims=((1,), (0,))):
    return lax.dot_general(
        left, right, (dims, ((), ())), precision=HIGHEST, preferred_element_type=jnp.float32
    )


def halves(value):
    high = value.astype(jnp.bfloat16)
    return high, (value - high.astype(jnp.float32)).astype(jnp.bfloat16)


def dot_halves(left, right, dims=((1,), (0,))):
    def one(a, b):
        return lax.dot_general(a, b, (dims, ((), ())), preferred_element_type=jnp.float32)

    return one(left[0], right[0]) + (one(left[0], right[1]) + one(left[1], right[0]))


def panel_step(panel, first, lane, sub, ones):
    cols = [across(panel, first + j) * ones for j in range(PANEL)]
    entry = [[None] * PANEL for _ in range(PANEL)]
    for i in range(PANEL):
        for j in range(i, PANEL):
            entry[i][j] = entry[j][i] = down(cols[j], i)
    inside = (lane >= first) & (lane < first + PANEL)
    augmented = jnp.where(inside, jnp.where(lane == first + sub, 1.0, 0.0), panel)
    lower = jnp.where(lane < first + PANEL, augmented, 0.0)
    rows = [down(augmented, i) for i in range(PANEL)]
    for j in range(0, PANEL, 2):
        p, b, s = entry[j][j], entry[j][j + 1], entry[j + 1][j + 1]
        r = 1.0 / (p * s - b * b)
        upper_new, lower_new = {}, {}
        for m in range(j + 2, PANEL):
            upper_new[m] = (s * entry[j][m] - b * entry[j + 1][m]) * r
            lower_new[m] = (p * entry[j + 1][m] - b * entry[j][m]) * r
        upper_row = (s * rows[j] - b * rows[j + 1]) * r
        lower_row = (p * rows[j + 1] - b * rows[j]) * r
        for i in range(PANEL):
            if i in (j, j + 1):
                continue
            f, g = entry[i][j], entry[i][j + 1]
            for m in range(max(j + 2, i if i > j else 0), PANEL):
                value = entry[i][m] - (f * upper_new[m] + g * lower_new[m])
                entry[i][m] = value
                if i > j and m > i:
                    entry[m][i] = value
            rows[i] = rows[i] - (f * upper_row + g * lower_row)
        for m in range(j + 2, PANEL):
            entry[j][m] = upper_new[m]
            entry[j + 1][m] = lower_new[m]
        rows[j], rows[j + 1] = upper_row, lower_row
    solved = rows[0]
    for i in range(1, PANEL):
        solved = jnp.where(sub == i, rows[i], solved)
    return lower, rows, solved, inside


def factor_block(block, lower_ref, scaled_ref, ones):
    count = BLOCK // PANEL
    lane = lax.broadcasted_iota(jnp.int32, (PANEL, BLOCK), 1)
    sub = lax.broadcasted_iota(jnp.int32, (PANEL, BLOCK), 0)
    rows = [block[PANEL * i : PANEL * (i + 1), :] for i in range(count)]
    for q in range(count):
        first = q * PANEL
        lower, pivot_rows, solved, inside = panel_step(rows[q], first, lane, sub, ones)
        lower_ref[first : first + PANEL, :] = lower
        scaled_ref[first : first + PANEL, :] = jnp.where(lane < first + PANEL, solved, 0.0)
        for i in range(q + 1, count):
            change = tree_sum(
                across(rows[i], first + j) * pivot_rows[j] for j in range(PANEL)
            )
            rows[i] = jnp.where(inside, 0.0, rows[i]) - change


def solve_kernel(diag_ref, rows_ref, out_ref, work_ref, lower_ref, scaled_ref, ones_ref):
    blocks = diag_ref.shape[0] // BLOCK
    ones_ref[...] = jnp.ones_like(ones_ref)
    ones = ones_ref[...]
    work_ref[...] = diag_ref[...]
    out_ref[...] = rows_ref[...]
    current = diag_ref[0:BLOCK, 0:BLOCK]
    for p in range(blocks):
        at, after = p * BLOCK, (p + 1) * BLOCK
        last = p == blocks - 1
        slot = p % 2
        factor_block(current, lower_ref.at[slot], scaled_ref.at[slot], ones)
        lower, scaled = lower_ref[slot], scaled_ref[slot]
        if not last:
            below = dot32(work_ref[after : after + BLOCK, at:after], lower, ((1,), (1,)))
            beside = dot32(scaled, work_ref[at:after, after : after + BLOCK])
            current = work_ref[after : after + BLOCK, after : after + BLOCK] - dot32(below, beside)
        inverse = halves(dot32(lower, scaled, ((0,), (0,))))
        if not last:
            panel = dot_halves(inverse, halves(work_ref[at:after, after:]))
            panel_parts = halves(panel)
        turned = dot_halves(halves(out_ref[:, at:after]), inverse)
        turned_parts = halves(turned)
        for i in range(blocks):
            if i == p:
                continue
            span = slice(i * BLOCK, (i + 1) * BLOCK)
            column = halves(work_ref[span, at:after])
            if not last:
                work_ref[span, after:] -= dot_halves(column, panel_parts)
            out_ref[:, span] -= dot_halves(turned_parts, column, ((1,), (1,)))
        if not last:
            work_ref[at:after, after:] = panel
        out_ref[:, at:after] = turned


def solve(diag, rows):
    count, nodes = rows.shape
    assert nodes % BLOCK == 0, nodes
    whole = pl.BlockSpec(memory_space=pltpu.VMEM)
    return pl.pallas_call(
        solve_kernel,
        out_shape=jax.ShapeDtypeStruct((count, nodes), jnp.float32),
        in_specs=[whole, whole],
        out_specs=whole,
        scratch_shapes=[
            pltpu.VMEM((nodes, nodes), jnp.float32),
            pltpu.VMEM((2, BLOCK, BLOCK), jnp.float32),
            pltpu.VMEM((2, BLOCK, BLOCK), jnp.float32),
            pltpu.VMEM((PANEL, BLOCK), jnp.float32),
        ],
        cost_estimate=pl.CostEstimate(
            flops=60 * nodes * nodes * nodes, bytes_accessed=4 * nodes * nodes, transcendentals=0
        ),
        name="solve_spd",
    )(diag, rows)


SPARE = 16
GROUP = ("space", "obs")


def shift(value, axis, steps, sources=None):
    count = lax.axis_size(axis)
    pairs = [
        (source, (source + steps) % count)
        for source in range(count)
        if sources is None or sources(source)
    ]
    return lax.ppermute(value, axis, pairs)


def rounded(value):
    return lax.reduce_precision(value, 8, 7)


def pieces_of(vector, count):
    parts = []
    for _ in range(count):
        part = rounded(vector)
        parts.append(part)
        vector = vector - part
    return parts


def own_diagonal(rows):
    count, nodes = rows.shape
    first = lax.axis_index(GROUP) * count
    row_at = lax.broadcasted_iota(jnp.int32, (count, nodes), 0) + first
    return row_at == lax.broadcasted_iota(jnp.int32, (count, nodes), 1)


def pack(rows, vectors=()):
    nodes = rows.shape[1]
    high = rounded(rows)
    rest = jnp.sum(jnp.where(own_diagonal(rows), rows - high, 0.0), axis=0)
    spare = [rest]
    for vector in vectors:
        for part in pieces_of(vector, 3):
            spare.append(jnp.pad(part, (0, nodes - part.shape[0])))
    spare += [jnp.zeros_like(rest)] * (SPARE - len(spare))
    return jnp.concatenate([high, jnp.stack(spare)], axis=0).astype(jnp.bfloat16)


def unpack_rows(packed):
    count = packed.shape[0] - SPARE
    rows = packed[:count].astype(jnp.float32)
    return rows + jnp.where(own_diagonal(rows), packed[count].astype(jnp.float32)[None, :], 0.0)


def unpack_vector(packed, length, at=0):
    first = packed.shape[0] - SPARE + 1 + 3 * at
    parts = packed[first : first + 3, :length].astype(jnp.float32)
    return parts[0] + (parts[1] + parts[2])


def place(pieces):
    n_space, n_obs = lax.axis_size("space"), lax.axis_size("obs")
    my_space, my_obs = lax.axis_index("space"), lax.axis_index("obs")
    first = pieces[0][2]
    whole = jnp.zeros((n_space * n_obs,) + first.shape, first.dtype)
    for space_shift, obs_shift, value in pieces:
        cell = lax.rem(my_space - space_shift + n_space, n_space) * n_obs + lax.rem(
            my_obs - obs_shift + n_obs, n_obs
        )
        whole = lax.dynamic_update_index_in_dim(whole, value, cell, 0)
    return whole


def spread(value):
    n_space, n_obs = lax.axis_size("space"), lax.axis_size("obs")
    along = [value] + [shift(value, "space", d) for d in range(1, n_space)]
    pieces = [(d, 0, part) for d, part in enumerate(along)]
    stacked = jnp.stack(along)
    for e in range(1, n_obs):
        got = shift(stacked, "obs", e)
        pieces += [(d, e, got[d]) for d in range(n_space)]
    return place(pieces)


def spread_at_once(value):
    n_space, n_obs = lax.axis_size("space"), lax.axis_size("obs")
    pieces = [(0, 0, value)]
    for d in range(n_space):
        for e in range(n_obs):
            if d == 0 and e == 0:
                continue
            pairs = [
                (s * n_obs + o, ((s + d) % n_space) * n_obs + (o + e) % n_obs)
                for s in range(n_space)
                for o in range(n_obs)
            ]
            pieces.append((d, e, lax.ppermute(value, GROUP, pairs)))
    return place(pieces)


def whole_rows(cells, first, count):
    return cells[:, first : first + count].reshape(-1, cells.shape[-1])


def whole_diagonal(cells, at):
    return jnp.sum(cells[:, at].astype(jnp.float32), axis=0)


def whole_vector(cells, first, length):
    parts = cells[:, first : first + 3, :length].astype(jnp.float32)
    return (parts[:, 0] + (parts[:, 1] + parts[:, 2])).reshape(-1)


def times(solved, partner_rows, partner_rest):
    high = rounded(solved)
    low = rounded(solved - high)

    def one(part):
        return lax.dot_general(
            part.astype(jnp.bfloat16),
            partner_rows,
            (((1,), (1,)), ((), ())),
            preferred_element_type=jnp.float32,
        )

    return one(high) + one(low) + solved * partner_rest[None, :]


def local(obs_panel, node_index, weight, residual, route_time, spatial_prec, ar_coef, prior_rhs):
    n_times = lax.axis_size("tm")
    time_index = lax.axis_index("tm")
    cell_index = lax.axis_index(GROUP)
    rows_dev, nodes = obs_panel.shape
    count = spatial_prec.shape[1]
    capacity = 2 * rows_dev // n_times

    def is_odd(time):
        return time % 2 == 1

    own_prec, own_coef, own_prior = spatial_prec[0], ar_coef[0], prior_rhs[0]
    from_next = shift(pack(own_prec, (ar_coef,)), "tm", -1)
    next_coef = unpack_vector(from_next, 1)[0]
    own_cells = spread(pack(own_prec, (own_prior,)))
    next_cells = spread(from_next)

    root = jnp.sqrt(weight.astype(jnp.float32))
    node_hits = node_index[:, None] == lax.iota(jnp.int32, nodes)[None, :]
    design = rounded(obs_panel.astype(jnp.float32) + node_hits.astype(jnp.float32))
    scaled = (root[:, None] * design).astype(jnp.bfloat16)
    target = root * residual.astype(jnp.float32)
    same = route_time[:, None] == route_time[None, :]
    earlier = lax.iota(jnp.int32, rows_dev)[:, None] > lax.iota(jnp.int32, rows_dev)[None, :]
    rank = jnp.sum((same & earlier).astype(jnp.int32), axis=1)
    slot_of = (
        (route_time[None, :, None] == lax.iota(jnp.int32, n_times)[:, None, None])
        & (rank[None, :, None] == lax.iota(jnp.int32, capacity)[None, None, :])
    ).astype(jnp.bfloat16)
    extra = jnp.stack(pieces_of(target, 2) + [jnp.zeros_like(target)] * (SPARE - 2), axis=1)
    send = lax.dot_general(
        jnp.broadcast_to(
            jnp.concatenate([scaled, extra.astype(jnp.bfloat16)], axis=1),
            (n_times, rows_dev, nodes + SPARE),
        ),
        slot_of,
        (((1,), (1,)), ((0,), (0,))),
        preferred_element_type=jnp.float32,
    ).astype(jnp.bfloat16)
    arrived = lax.all_to_all(send, "tm", split_axis=0, concat_axis=0, tiled=True)

    def moments(slots):
        flat = jnp.concatenate([slots[i] for i in range(slots.shape[0])], axis=1)
        return lax.dot_general(
            flat[:nodes], flat, (((1,), (1,)), ((), ())), preferred_element_type=jnp.float32
        )

    n_space, n_obs = lax.axis_size("space"), lax.axis_size("obs")
    near = [arrived] + [shift(arrived, "obs", e) for e in range(1, n_obs)]
    far = [shift(arrived, "space", d) for d in range(1, n_space)]
    far += [shift(part, "obs", e) for e in range(1, n_obs) for part in far]
    sums = moments(jnp.concatenate(near, axis=0))
    if far:
        sums = sums + moments(jnp.concatenate(far, axis=0))
    gram = sums[:, :nodes]
    grad = sums[:, nodes] + sums[:, nodes + 1]

    own_high = whole_rows(own_cells, 0, count)
    own_rest = whole_diagonal(own_cells, count)
    next_high = whole_rows(next_cells, 0, count)
    next_rest = whole_diagonal(next_cells, count)
    square = next_coef * next_coef
    eye = lax.iota(jnp.int32, nodes)[:, None] == lax.iota(jnp.int32, nodes)[None, :]
    diag_full = (
        own_high.astype(jnp.float32)
        + square * next_high.astype(jnp.float32)
        + jnp.where(eye, (own_rest + square * next_rest)[None, :], 0.0)
        + gram
    )
    rhs_full = whole_vector(own_cells, count + 1, count) + grad
    next_prec = unpack_rows(from_next)
    first_row = cell_index * count
    diag_one = own_prec + square * next_prec + lax.dynamic_slice_in_dim(gram, first_row, count, 0)
    rhs_one = own_prior + lax.dynamic_slice_in_dim(grad, first_row, count, 0)
    solved = solve(
        diag_full, jnp.concatenate([-own_coef * own_prec, -next_coef * next_prec], axis=0)
    )
    left_product = -own_coef * times(solved, own_high, own_rest)
    right_product = -next_coef * times(solved, next_high, next_rest)
    up = jnp.sum(solved * rhs_full[None, :], axis=1)
    loss_left, loss_right = left_product[:count], right_product[count:]
    fill_one, turn_one = -right_product[:count], -left_product[count:]
    up_left, up_right = up[:count], up[count:]

    packed_left, packed_right = pack(loss_left, (up_left,)), pack(loss_right, (up_right,))
    go_right = jnp.concatenate([packed_right, pack(fill_one)], axis=0)
    go_left = jnp.concatenate([packed_left, pack(turn_one)], axis=0)
    size = count + SPARE
    came_left = shift(go_right, "tm", 1, lambda time: time % 4 == 1)
    came_right = shift(go_left, "tm", -1, lambda time: time % 4 == 3)
    late_left, late_right = lax.optimization_barrier(
        ((packed_right, packed_left), came_left, came_right)
    )[0]
    late_left = shift(late_left, "tm", 1, lambda time: time % 4 == 3)
    late_right = shift(late_right, "tm", -1, lambda time: time % 4 == 1)

    diag_two = diag_one - unpack_rows(came_left[:size]) - unpack_rows(came_right[:size])
    rhs_two = (
        rhs_one
        - unpack_vector(came_left[:size], count)
        - unpack_vector(came_right[:size], count)
    )
    diag_cells = spread(pack(diag_two, (rhs_two,)))
    partner = jnp.concatenate([came_left[size:], came_right[size:]], axis=0)
    partner_cells = spread_at_once(partner)
    diag_full = whole_rows(diag_cells, 0, count).astype(jnp.float32) + jnp.where(
        eye, whole_diagonal(diag_cells, count)[None, :], 0.0
    )
    rhs_full = whole_vector(diag_cells, count + 1, count)
    solved = solve(
        diag_full,
        jnp.concatenate([unpack_rows(partner[:size]), unpack_rows(partner[size:])], axis=0),
    )
    left_product = times(
        solved, whole_rows(partner_cells, 0, count), whole_diagonal(partner_cells, count)
    )
    right_product = times(
        solved, whole_rows(partner_cells, size, count), whole_diagonal(partner_cells, size + count)
    )
    up = jnp.sum(solved * rhs_full[None, :], axis=1)
    fill_two = -right_product[:count]

    def is_second(time):
        return time % 4 == 2

    if 4 % n_times == 0:
        losses = pack(
            left_product[:count] + right_product[count:], (up[:count] + up[count:],)
        )
        came = [shift(losses, "tm", 2, is_second)]
    else:
        came = [
            shift(pack(left_product[:count], (up[:count],)), "tm", -2, is_second),
            shift(pack(right_product[count:], (up[count:],)), "tm", 2, is_second),
        ]
    diag_out = diag_two - unpack_rows(late_left) - unpack_rows(late_right)
    rhs_out = rhs_two - unpack_vector(late_left, count) - unpack_vector(late_right, count)
    for part in came:
        diag_out = diag_out - unpack_rows(part)
        rhs_out = rhs_out - unpack_vector(part, count)
    fill_out = jnp.where(
        is_odd(time_index),
        fill_one,
        jnp.where(is_second(time_index), fill_two, jnp.zeros_like(fill_two)),
    )
    return (diag_out[None], fill_out[None], rhs_out[None])


def solution(mesh):
    return jax.shard_map(
        local,
        mesh=mesh,
        in_specs=(
            P(("grp", "tm", "space", "obs"), None),
            P(("grp", "tm", "space", "obs")),
            P(("grp", "tm", "space", "obs")),
            P(("grp", "tm", "space", "obs")),
            P(("grp", "tm", "space", "obs")),
            P(("grp", "tm"), ("space", "obs"), None),
            P(("grp", "tm")),
            P(("grp", "tm"), ("space", "obs")),
        ),
        out_specs=(
            P(("grp", "tm"), ("space", "obs"), None),
            P(("grp", "tm"), ("space", "obs"), None),
            P(("grp", "tm"), ("space", "obs")),
        ),
        check_vma=False,
    )
```

```python
import functools

import jax
import jax.numpy as jnp
from jax import lax
from jax.experimental import pallas as pl
from jax.experimental.pallas import tpu as pltpu
from jax.sharding import PartitionSpec as P


BLOCK = 128
PANEL = 8
HIGHEST = lax.Precision.HIGHEST


def across(value, lane_index):
    return jnp.broadcast_to(value[:, lane_index : lane_index + 1], value.shape)


def down(value, row_index):
    return jnp.broadcast_to(value[row_index : row_index + 1, :], value.shape)


def tree_sum(terms):
    terms = list(terms)
    while len(terms) > 1:
        terms = [
            terms[at] + terms[at + 1] if at + 1 < len(terms) else terms[at]
            for at in range(0, len(terms), 2)
        ]
    return terms[0]


def dot32(left, right, dims=((1,), (0,))):
    return lax.dot_general(
        left, right, (dims, ((), ())), precision=HIGHEST, preferred_element_type=jnp.float32
    )


def halves(value):
    high = value.astype(jnp.bfloat16)
    return high, (value - high.astype(jnp.float32)).astype(jnp.bfloat16)


def dot_halves(left, right, dims=((1,), (0,))):
    def one(a, b):
        return lax.dot_general(a, b, (dims, ((), ())), preferred_element_type=jnp.float32)

    return one(left[0], right[0]) + (one(left[0], right[1]) + one(left[1], right[0]))


def panel_step(panel, first, lane, sub, ones):
    cols = [across(panel, first + j) * ones for j in range(PANEL)]
    entry = [[None] * PANEL for _ in range(PANEL)]
    for i in range(PANEL):
        for j in range(i, PANEL):
            entry[i][j] = entry[j][i] = down(cols[j], i)
    inside = (lane >= first) & (lane < first + PANEL)
    augmented = jnp.where(inside, jnp.where(lane == first + sub, 1.0, 0.0), panel)
    lower = jnp.where(lane < first + PANEL, augmented, 0.0)
    rows = [down(augmented, i) for i in range(PANEL)]
    for j in range(0, PANEL, 2):
        p, b, s = entry[j][j], entry[j][j + 1], entry[j + 1][j + 1]
        r = 1.0 / (p * s - b * b)
        upper_new, lower_new = {}, {}
        for m in range(j + 2, PANEL):
            upper_new[m] = (s * entry[j][m] - b * entry[j + 1][m]) * r
            lower_new[m] = (p * entry[j + 1][m] - b * entry[j][m]) * r
        upper_row = (s * rows[j] - b * rows[j + 1]) * r
        lower_row = (p * rows[j + 1] - b * rows[j]) * r
        for i in range(PANEL):
            if i in (j, j + 1):
                continue
            f, g = entry[i][j], entry[i][j + 1]
            for m in range(max(j + 2, i if i > j else 0), PANEL):
                value = entry[i][m] - (f * upper_new[m] + g * lower_new[m])
                entry[i][m] = value
                if i > j and m > i:
                    entry[m][i] = value
            rows[i] = rows[i] - (f * upper_row + g * lower_row)
        for m in range(j + 2, PANEL):
            entry[j][m] = upper_new[m]
            entry[j + 1][m] = lower_new[m]
        rows[j], rows[j + 1] = upper_row, lower_row
    solved = rows[0]
    for i in range(1, PANEL):
        solved = jnp.where(sub == i, rows[i], solved)
    return lower, rows, solved, inside


def factor_block(block, lower_ref, scaled_ref, ones):
    count = BLOCK // PANEL
    lane = lax.broadcasted_iota(jnp.int32, (PANEL, BLOCK), 1)
    sub = lax.broadcasted_iota(jnp.int32, (PANEL, BLOCK), 0)
    rows = [block[PANEL * i : PANEL * (i + 1), :] for i in range(count)]
    for q in range(count):
        first = q * PANEL
        lower, pivot_rows, solved, inside = panel_step(rows[q], first, lane, sub, ones)
        lower_ref[first : first + PANEL, :] = lower
        scaled_ref[first : first + PANEL, :] = jnp.where(lane < first + PANEL, solved, 0.0)
        for i in range(q + 1, count):
            change = tree_sum(
                across(rows[i], first + j) * pivot_rows[j] for j in range(PANEL)
            )
            rows[i] = jnp.where(inside, 0.0, rows[i]) - change


SPARE = 16
GROUP = ("space", "obs")


def gauss_jordan(work_ref, out_ref, lower_ref, scaled_ref, ones_ref):
    blocks = work_ref.shape[0] // BLOCK
    ones_ref[...] = jnp.ones_like(ones_ref)
    ones = ones_ref[...]
    current = work_ref[0:BLOCK, 0:BLOCK]
    for p in range(blocks):
        at, after = p * BLOCK, (p + 1) * BLOCK
        last = p == blocks - 1
        slot = p % 2
        factor_block(current, lower_ref.at[slot], scaled_ref.at[slot], ones)
        lower, scaled = lower_ref[slot], scaled_ref[slot]
        if not last:
            below = dot32(work_ref[after : after + BLOCK, at:after], lower, ((1,), (1,)))
            beside = dot32(scaled, work_ref[at:after, after : after + BLOCK])
            current = work_ref[after : after + BLOCK, after : after + BLOCK] - dot32(below, beside)
        inverse = halves(dot32(lower, scaled, ((0,), (0,))))
        if not last:
            panel = dot_halves(inverse, halves(work_ref[at:after, after:]))
            panel_parts = halves(panel)
        turned = dot_halves(halves(out_ref[:, at:after]), inverse)
        turned_parts = halves(turned)
        for i in range(blocks):
            if i == p:
                continue
            span = slice(i * BLOCK, (i + 1) * BLOCK)
            column = halves(work_ref[span, at:after])
            if not last:
                work_ref[span, after:] -= dot_halves(column, panel_parts)
            out_ref[:, span] -= dot_halves(turned_parts, column, ((1,), (1,)))
        if not last:
            work_ref[at:after, after:] = panel
        out_ref[:, at:after] = turned


def diagonal_mask(count, nodes, first):
    row_at = lax.broadcasted_iota(jnp.int32, (count, nodes), 0) + first
    return row_at == lax.broadcasted_iota(jnp.int32, (count, nodes), 1)


def to_row(column, mask):
    return jnp.sum(jnp.where(mask, column, 0.0), axis=0, keepdims=True)


def write_packed(ref, start, rows, mask, vectors):
    count, nodes = rows.shape
    high = rows.astype(jnp.bfloat16)
    ref[start : start + count, :] = high
    lines = [to_row(rows - high.astype(jnp.float32), mask)]
    for vector in vectors:
        for _ in range(3):
            part = vector.astype(jnp.bfloat16).astype(jnp.float32)
            lines.append(part)
            vector = vector - part
    place = lax.broadcasted_iota(jnp.int32, (SPARE, nodes), 0)
    spare = jnp.zeros((SPARE, nodes), jnp.float32)
    for at, line in enumerate(lines):
        spare = jnp.where(place == at, jnp.broadcast_to(line, spare.shape), spare)
    ref[start + count : start + count + SPARE, :] = spare.astype(jnp.bfloat16)


def read_spare(ref, start, count):
    return ref[start + count : start + count + SPARE, :].astype(jnp.float32)


def spare_vector(spare, at):
    first = 1 + 3 * at
    return spare[first : first + 1] + (
        spare[first + 1 : first + 2] + spare[first + 2 : first + 3]
    )


def read_rows(ref, start, count, mask):
    rows = ref[start : start + count, :].astype(jnp.float32)
    return rows + jnp.where(mask, read_spare(ref, start, count)[0:1], 0.0)


def partner_product(solved, partner_ref, rest):
    high, low = halves(solved)

    def one(part):
        return lax.dot_general(
            part, partner_ref[...], (((1,), (1,)), ((), ())), preferred_element_type=jnp.float32
        )

    return one(high) + one(low) + solved * rest


def pack_kernel(cells_ref, rows_ref, coef_ref, prior_ref, out_ref):
    count, nodes = rows_ref.shape
    mask = diagonal_mask(count, nodes, cells_ref[0] * count)
    lane = lax.broadcasted_iota(jnp.int32, (1, nodes), 1)
    coef = jnp.where(lane == 0, jnp.broadcast_to(coef_ref[...], (1, nodes)), 0.0)
    prior = to_row(jnp.broadcast_to(prior_ref[...], (count, nodes)), mask)
    write_packed(out_ref, 0, rows_ref[...], mask, (coef, prior))


def first_kernel(n_cells, cells_ref, coef_ref, prec_ref, gram_ref, *refs):
    own_refs, next_refs = refs[:n_cells], refs[n_cells : 2 * n_cells]
    go_right, go_left, fill_ref, diag_ref, rhs_ref = refs[2 * n_cells : 2 * n_cells + 5]
    work_ref, out_ref, own_all, next_all, lower_ref, scaled_ref, ones_ref = refs[
        2 * n_cells + 5 :
    ]
    count, nodes = prec_ref.shape
    own_coef = coef_ref[...]
    next_spare = read_spare(next_refs[0], 0, count)
    next_coef = spare_vector(next_spare, 0)[:, 0:1]
    square = next_coef * next_coef
    own_rest = jnp.zeros((1, nodes), jnp.float32)
    next_rest = jnp.zeros((1, nodes), jnp.float32)
    rhs = gram_ref[nodes : nodes + 1, :] + gram_ref[nodes + 1 : nodes + 2, :]
    for k in range(n_cells):
        first = pl.multiple_of(cells_ref[k] * count, SPARE)
        span = pl.ds(first, count)
        mask = diagonal_mask(count, nodes, first)
        own_spare = read_spare(own_refs[k], 0, count)
        own_rest = own_rest + own_spare[0:1]
        next_rest = next_rest + read_spare(next_refs[k], 0, count)[0:1]
        prior = spare_vector(own_spare, 1)
        rhs = rhs + prior
        own_high, next_high = own_refs[k][0:count, :], next_refs[k][0:count, :]
        own_all[span, :] = own_high
        next_all[span, :] = next_high
        own_rows = read_rows(own_refs[k], 0, count, mask)
        next_rows = read_rows(next_refs[k], 0, count, mask)
        if k == 0:
            own_rows = prec_ref[...]
        rows = own_rows + square * next_rows + gram_ref[span, :]
        work_ref[span, :] = rows
        if k == 0:
            my_mask = mask
            diag_ref[...] = rows
            out_ref[0:count, :] = -own_coef * own_rows
            out_ref[count : 2 * count, :] = -next_coef * next_rows
    my_columns = jnp.sum(jnp.where(my_mask, 1.0, 0.0), axis=0, keepdims=True)
    rhs_ref[...] = jnp.broadcast_to(jnp.where(my_columns > 0.5, rhs, 0.0), rhs_ref.shape)
    gauss_jordan(work_ref, out_ref, lower_ref, scaled_ref, ones_ref)
    solved = out_ref[...]
    up = jnp.sum(solved * rhs, axis=1, keepdims=True)
    left = -own_coef * partner_product(solved, own_all, own_rest)
    right = -next_coef * partner_product(solved, next_all, next_rest)
    size = count + SPARE
    up_left, up_right = to_row(up[:count], my_mask), to_row(up[count:], my_mask)
    write_packed(go_right, 0, right[count:], my_mask, (up_right,))
    write_packed(go_right, size, -right[:count], my_mask, ())
    write_packed(go_left, 0, left[:count], my_mask, (up_left,))
    write_packed(go_left, size, -left[count:], my_mask, ())
    fill_ref[...] = -right[:count]


def merge_kernel(cells_ref, diag_ref, rhs_ref, left_ref, right_ref, pack_ref, out_ref, out_rhs):
    count, nodes = diag_ref.shape
    mask = diagonal_mask(count, nodes, cells_ref[0] * count)
    rows = (
        diag_ref[...] - read_rows(left_ref, 0, count, mask) - read_rows(right_ref, 0, count, mask)
    )
    rhs = (
        rhs_ref[0:1]
        - spare_vector(read_spare(left_ref, 0, count), 0)
        - spare_vector(read_spare(right_ref, 0, count), 0)
    )
    out_ref[...] = rows
    out_rhs[...] = jnp.broadcast_to(rhs, out_rhs.shape)
    write_packed(pack_ref, 0, rows, mask, (rhs,))


def second_kernel(n_cells, cells_ref, left_ref, right_ref, *refs):
    diag_refs = refs[:n_cells]
    out_ref, rhs_ref, work_ref, lower_ref, scaled_ref, ones_ref = refs[n_cells:]
    count = diag_refs[0].shape[0] - SPARE
    nodes = diag_refs[0].shape[1]
    size = count + SPARE
    rhs = jnp.zeros((1, nodes), jnp.float32)
    for k in range(n_cells):
        first = pl.multiple_of(cells_ref[k] * count, SPARE)
        mask = diagonal_mask(count, nodes, first)
        work_ref[pl.ds(first, count), :] = read_rows(diag_refs[k], 0, count, mask)
        rhs = rhs + spare_vector(read_spare(diag_refs[k], 0, count), 0)
        if k == 0:
            out_ref[0:count, :] = read_rows(left_ref, size, count, mask)
            out_ref[count : 2 * count, :] = read_rows(right_ref, size, count, mask)
    rhs_ref[...] = jnp.broadcast_to(rhs, rhs_ref.shape)
    gauss_jordan(work_ref, out_ref, lower_ref, scaled_ref, ones_ref)


def last_kernel(n_cells, together, cells_ref, solved_ref, rhs_ref, *refs):
    pieces = refs[: n_cells + 1]
    loss_ref, fill_ref, left_all, right_all = refs[n_cells + 1 :]
    nodes = solved_ref.shape[1]
    count = solved_ref.shape[0] // 2
    size = count + SPARE
    rests = [jnp.zeros((1, nodes), jnp.float32), jnp.zeros((1, nodes), jnp.float32)]
    for k in range(n_cells):
        span = pl.ds(pl.multiple_of(cells_ref[k] * count, SPARE), count)
        sources = [(pieces[0], size), (pieces[1], size)]
        if k:
            sources = [(pieces[k + 1], 0), (pieces[k + 1], size)]
        for side, (ref, start) in enumerate(sources):
            (left_all, right_all)[side][span, :] = ref[start : start + count, :]
            rests[side] = rests[side] + read_spare(ref, start, count)[0:1]
    mask = diagonal_mask(count, nodes, cells_ref[0] * count)
    solved = solved_ref[...]
    up = jnp.sum(solved * rhs_ref[0:1], axis=1, keepdims=True)
    up_left, up_right = to_row(up[:count], mask), to_row(up[count:], mask)
    left = partner_product(solved[:count], left_all, rests[0])
    right = partner_product(solved, right_all, rests[1])
    if together:
        write_packed(loss_ref, 0, left + right[count:], mask, (up_left + up_right,))
    else:
        write_packed(loss_ref, 0, left, mask, (up_left,))
        write_packed(loss_ref, size, right[count:], mask, (up_right,))
    fill_ref[...] = -right[:count]


def on_chip(kernel, name, out_shapes, scratch, operands, flops):
    vmem = pl.BlockSpec(memory_space=pltpu.VMEM)
    cells = pl.BlockSpec(memory_space=pltpu.SMEM)
    return pl.pallas_call(
        kernel,
        out_shape=[jax.ShapeDtypeStruct(shape, dtype) for shape, dtype in out_shapes],
        in_specs=[cells] + [vmem] * (len(operands) - 1),
        out_specs=[vmem] * len(out_shapes),
        scratch_shapes=[pltpu.VMEM(shape, dtype) for shape, dtype in scratch],
        cost_estimate=pl.CostEstimate(flops=flops, bytes_accessed=1 << 20, transcendentals=0),
        name=name,
    )(*operands)


def solve_scratch():
    return [
        ((2, BLOCK, BLOCK), jnp.float32),
        ((2, BLOCK, BLOCK), jnp.float32),
        ((PANEL, BLOCK), jnp.float32),
    ]


def shift(value, axis, steps, sources=None):
    count = lax.axis_size(axis)
    pairs = [
        (source, (source + steps) % count)
        for source in range(count)
        if sources is None or sources(source)
    ]
    return lax.ppermute(value, axis, pairs)


def cell_shifts():
    n_space, n_obs = lax.axis_size("space"), lax.axis_size("obs")
    return [(d, e) for e in range(n_obs) for d in range(n_space)]


def cell_table():
    n_space, n_obs = lax.axis_size("space"), lax.axis_size("obs")
    my_space, my_obs = lax.axis_index("space"), lax.axis_index("obs")
    cells = [
        lax.rem(my_space - d + n_space, n_space) * n_obs + lax.rem(my_obs - e + n_obs, n_obs)
        for d, e in cell_shifts()
    ]
    return jnp.stack(cells).astype(jnp.int32)


def spread(value):
    n_space, n_obs = lax.axis_size("space"), lax.axis_size("obs")
    along = [value] + [shift(value, "space", d) for d in range(1, n_space)]
    pieces = list(along)
    for e in range(1, n_obs):
        pieces += [shift(part, "obs", e) for part in along]
    return pieces


def spread_at_once(value):
    n_space, n_obs = lax.axis_size("space"), lax.axis_size("obs")
    pieces = []
    for d, e in cell_shifts()[1:]:
        pairs = [
            (s * n_obs + o, ((s + d) % n_space) * n_obs + (o + e) % n_obs)
            for s in range(n_space)
            for o in range(n_obs)
        ]
        pieces.append(lax.ppermute(value, GROUP, pairs))
    return pieces


def rounded(value):
    return lax.reduce_precision(value, 8, 7)


def unpack_rows(packed, mask):
    count = packed.shape[0] - SPARE
    rows = packed[:count].astype(jnp.float32)
    return rows + jnp.where(mask, packed[count].astype(jnp.float32)[None, :], 0.0)


def unpack_vector(packed):
    first = packed.shape[0] - SPARE + 1
    parts = packed[first : first + 3].astype(jnp.float32)
    return parts[0] + (parts[1] + parts[2])


def routed_rows(obs_panel, node_index, weight, residual, route_time, n_times):
    rows_dev, nodes = obs_panel.shape
    capacity = 2 * rows_dev // n_times
    root = jnp.sqrt(weight.astype(jnp.float32))
    node_hits = node_index[:, None] == lax.iota(jnp.int32, nodes)[None, :]
    design = rounded(obs_panel.astype(jnp.float32) + node_hits.astype(jnp.float32))
    scaled = (root[:, None] * design).astype(jnp.bfloat16)
    target = root * residual.astype(jnp.float32)
    target_high = rounded(target)
    same = route_time[:, None] == route_time[None, :]
    earlier = lax.iota(jnp.int32, rows_dev)[:, None] > lax.iota(jnp.int32, rows_dev)[None, :]
    rank = jnp.sum((same & earlier).astype(jnp.int32), axis=1)
    ahead = lax.rem(route_time - lax.axis_index("tm") + n_times, n_times)
    column = lax.iota(jnp.int32, SPARE)[None, :]
    extra = jnp.where(
        column == 0,
        target_high[:, None],
        jnp.where(column == 1, (target - target_high)[:, None], 0.0),
    ).astype(jnp.bfloat16)
    rows = jnp.concatenate([scaled, extra], axis=1)
    slots = lax.iota(jnp.int32, capacity)[None, :]
    parts = []
    for step in range(n_times):
        slot_of = (ahead[:, None] == step) & (rank[:, None] == slots)
        part = lax.dot_general(
            rows,
            slot_of.astype(jnp.bfloat16),
            (((0,), (0,)), ((), ())),
            preferred_element_type=jnp.float32,
        ).astype(jnp.bfloat16)
        parts.append(shift(part, "tm", step) if step else part)
    return parts


def moments(slots, nodes):
    return lax.dot_general(
        slots, slots[:nodes], (((1,), (1,)), ((), ())), preferred_element_type=jnp.float32
    )


def local(obs_panel, node_index, weight, residual, route_time, spatial_prec, ar_coef, prior_rhs):
    n_times = lax.axis_size("tm")
    n_space, n_obs = lax.axis_size("space"), lax.axis_size("obs")
    n_cells = n_space * n_obs
    time_index = lax.axis_index("tm")
    nodes = obs_panel.shape[1]
    count = spatial_prec.shape[1]
    size = count + SPARE
    assert nodes % BLOCK == 0 and count % SPARE == 0
    cells = cell_table()
    first_row = cells[0] * count
    own_prec, coef = spatial_prec[0], ar_coef.reshape(1, 1)
    (own_pack,) = on_chip(
        pack_kernel,
        "pack_prior",
        [((size, nodes), jnp.bfloat16)],
        [],
        (cells, own_prec, coef, prior_rhs.reshape(count, 1)),
        0,
    )
    own_pack, route_time = lax.optimization_barrier((own_pack, route_time))
    from_next = shift(own_pack, "tm", -1)
    own_pieces = spread(own_pack)
    parts = routed_rows(obs_panel, node_index, weight, residual, route_time, n_times)
    next_pieces = spread(from_next)
    parts, own_pieces[:n_space], next_pieces[:n_space] = lax.optimization_barrier(
        (parts, own_pieces[:n_space], next_pieces[:n_space])
    )
    arrived = jnp.concatenate(parts, axis=1)

    near = [arrived] + [shift(arrived, "obs", e) for e in range(1, n_obs)]
    far = [shift(arrived, "space", d) for d in range(1, n_space)]
    far += [shift(part, "obs", e) for e in range(1, n_obs) for part in far]
    gram = moments(near[0], nodes)
    for part in near[1:] + far:
        gram = gram + moments(part, nodes)

    go_right, go_left, fill_one, diag_one, rhs_one = on_chip(
        functools.partial(first_kernel, n_cells),
        "level_one",
        [
            ((2 * size, nodes), jnp.bfloat16),
            ((2 * size, nodes), jnp.bfloat16),
            ((count, nodes), jnp.float32),
            ((count, nodes), jnp.float32),
            ((8, nodes), jnp.float32),
        ],
        [
            ((nodes, nodes), jnp.float32),
            ((2 * count, nodes), jnp.float32),
            ((nodes, nodes), jnp.bfloat16),
            ((nodes, nodes), jnp.bfloat16),
        ]
        + solve_scratch(),
        (cells, coef, own_prec, gram, *own_pieces, *next_pieces),
        70 * nodes**3,
    )
    came_left = shift(go_right, "tm", 1, lambda time: time % 4 == 1)
    came_right = shift(go_left, "tm", -1, lambda time: time % 4 == 3)

    pack_two, diag_two, rhs_two = on_chip(
        merge_kernel,
        "merge_losses",
        [
            ((size, nodes), jnp.bfloat16),
            ((count, nodes), jnp.float32),
            ((8, nodes), jnp.float32),
        ],
        [],
        (cells, diag_one, rhs_one, came_left, came_right),
        0,
    )
    pieces_two = spread(pack_two)
    ready = pieces_two[1 % n_cells]
    partner, late_right_pack, late_left_pack, _ = lax.optimization_barrier(
        (
            jnp.concatenate([came_left[size:], came_right[size:]], axis=0),
            go_right[:size],
            go_left[:size],
            ready,
        )
    )
    partners = spread_at_once(partner)
    late_left = shift(late_right_pack, "tm", 1, lambda time: time % 4 == 3)
    late_right = shift(late_left_pack, "tm", -1, lambda time: time % 4 == 1)
    solved, rhs_full = on_chip(
        functools.partial(second_kernel, n_cells),
        "level_two",
        [((2 * count, nodes), jnp.float32), ((8, nodes), jnp.float32)],
        [((nodes, nodes), jnp.float32)] + solve_scratch(),
        (cells, came_left, came_right, *pieces_two),
        60 * nodes**3,
    )
    together = 4 % n_times == 0
    loss_two, fill_two = on_chip(
        functools.partial(last_kernel, n_cells, together),
        "products_two",
        [
            ((size if together else 2 * size, nodes), jnp.bfloat16),
            ((count, nodes), jnp.float32),
        ],
        [((nodes, nodes), jnp.bfloat16), ((nodes, nodes), jnp.bfloat16)],
        (cells, solved, rhs_full, came_left, came_right, *partners),
        4 * nodes**3,
    )

    def is_second(time):
        return time % 4 == 2

    if together:
        came = [shift(loss_two, "tm", 2, is_second)]
    else:
        came = [
            shift(loss_two[:size], "tm", -2, is_second),
            shift(loss_two[size:], "tm", 2, is_second),
        ]
    mask = diagonal_mask(count, nodes, first_row)
    diag_out = diag_two - unpack_rows(late_left, mask) - unpack_rows(late_right, mask)
    rhs_out = rhs_two[0] - unpack_vector(late_left) - unpack_vector(late_right)
    for part in came:
        diag_out = diag_out - unpack_rows(part, mask)
        rhs_out = rhs_out - unpack_vector(part)
    rhs_out = lax.dynamic_slice_in_dim(rhs_out, first_row, count, 0)
    fill_out = jnp.where(
        time_index % 2 == 1,
        fill_one,
        jnp.where(is_second(time_index), fill_two, jnp.zeros_like(fill_two)),
    )
    return (diag_out[None], fill_out[None], rhs_out[None])


def solution(mesh):
    return jax.shard_map(
        local,
        mesh=mesh,
        in_specs=(
            P(("grp", "tm", "space", "obs"), None),
            P(("grp", "tm", "space", "obs")),
            P(("grp", "tm", "space", "obs")),
            P(("grp", "tm", "space", "obs")),
            P(("grp", "tm", "space", "obs")),
            P(("grp", "tm"), ("space", "obs"), None),
            P(("grp", "tm")),
            P(("grp", "tm"), ("space", "obs")),
        ),
        out_specs=(
            P(("grp", "tm"), ("space", "obs"), None),
            P(("grp", "tm"), ("space", "obs"), None),
            P(("grp", "tm"), ("space", "obs")),
        ),
        check_vma=False,
    )
```

```python
import functools

import jax
import jax.numpy as jnp
from jax import lax
from jax.experimental import pallas as pl
from jax.experimental.pallas import tpu as pltpu
from jax.sharding import PartitionSpec as P


BLOCK = 128
PANEL = 8
HIGHEST = lax.Precision.HIGHEST


def across(value, lane_index):
    return jnp.broadcast_to(value[:, lane_index : lane_index + 1], value.shape)


def down(value, row_index):
    return jnp.broadcast_to(value[row_index : row_index + 1, :], value.shape)


def tree_sum(terms):
    terms = list(terms)
    while len(terms) > 1:
        terms = [
            terms[at] + terms[at + 1] if at + 1 < len(terms) else terms[at]
            for at in range(0, len(terms), 2)
        ]
    return terms[0]


def dot32(left, right, dims=((1,), (0,))):
    return lax.dot_general(
        left, right, (dims, ((), ())), precision=HIGHEST, preferred_element_type=jnp.float32
    )


def halves(value):
    high = value.astype(jnp.bfloat16)
    return high, (value - high.astype(jnp.float32)).astype(jnp.bfloat16)


def dot_halves(left, right, dims=((1,), (0,))):
    def one(a, b):
        return lax.dot_general(a, b, (dims, ((), ())), preferred_element_type=jnp.float32)

    return one(left[0], right[0]) + (one(left[0], right[1]) + one(left[1], right[0]))


def panel_step(panel, first, lane, sub, ones):
    cols = [across(panel, first + j) * ones for j in range(PANEL)]
    entry = [[None] * PANEL for _ in range(PANEL)]
    for i in range(PANEL):
        for j in range(i, PANEL):
            entry[i][j] = entry[j][i] = down(cols[j], i)
    inside = (lane >= first) & (lane < first + PANEL)
    augmented = jnp.where(inside, jnp.where(lane == first + sub, 1.0, 0.0), panel)
    lower = jnp.where(lane < first + PANEL, augmented, 0.0)
    rows = [down(augmented, i) for i in range(PANEL)]
    for j in range(0, PANEL, 2):
        p, b, s = entry[j][j], entry[j][j + 1], entry[j + 1][j + 1]
        r = 1.0 / (p * s - b * b)
        upper_new, lower_new = {}, {}
        for m in range(j + 2, PANEL):
            upper_new[m] = (s * entry[j][m] - b * entry[j + 1][m]) * r
            lower_new[m] = (p * entry[j + 1][m] - b * entry[j][m]) * r
        upper_row = (s * rows[j] - b * rows[j + 1]) * r
        lower_row = (p * rows[j + 1] - b * rows[j]) * r
        for i in range(PANEL):
            if i in (j, j + 1):
                continue
            f, g = entry[i][j], entry[i][j + 1]
            for m in range(max(j + 2, i if i > j else 0), PANEL):
                value = entry[i][m] - (f * upper_new[m] + g * lower_new[m])
                entry[i][m] = value
                if i > j and m > i:
                    entry[m][i] = value
            rows[i] = rows[i] - (f * upper_row + g * lower_row)
        for m in range(j + 2, PANEL):
            entry[j][m] = upper_new[m]
            entry[j + 1][m] = lower_new[m]
        rows[j], rows[j + 1] = upper_row, lower_row
    solved = rows[0]
    for i in range(1, PANEL):
        solved = jnp.where(sub == i, rows[i], solved)
    return lower, rows, solved, inside


def factor_block(block, lower_ref, scaled_ref, ones):
    count = BLOCK // PANEL
    lane = lax.broadcasted_iota(jnp.int32, (PANEL, BLOCK), 1)
    sub = lax.broadcasted_iota(jnp.int32, (PANEL, BLOCK), 0)
    rows = [block[PANEL * i : PANEL * (i + 1), :] for i in range(count)]
    for q in range(count):
        first = q * PANEL
        lower, pivot_rows, solved, inside = panel_step(rows[q], first, lane, sub, ones)
        lower_ref[first : first + PANEL, :] = lower
        scaled_ref[first : first + PANEL, :] = jnp.where(lane < first + PANEL, solved, 0.0)
        for i in range(q + 1, count):
            change = tree_sum(
                across(rows[i], first + j) * pivot_rows[j] for j in range(PANEL)
            )
            rows[i] = jnp.where(inside, 0.0, rows[i]) - change


SPARE = 16
GROUP = ("space", "obs")


def gauss_jordan(work_ref, out_ref, lower_ref, scaled_ref, ones_ref):
    blocks = work_ref.shape[0] // BLOCK
    ones_ref[...] = jnp.ones_like(ones_ref)
    ones = ones_ref[...]
    current = work_ref[0:BLOCK, 0:BLOCK]
    for p in range(blocks):
        at, after = p * BLOCK, (p + 1) * BLOCK
        last = p == blocks - 1
        slot = p % 2
        factor_block(current, lower_ref.at[slot], scaled_ref.at[slot], ones)
        lower, scaled = lower_ref[slot], scaled_ref[slot]
        if not last:
            below = dot32(work_ref[after : after + BLOCK, at:after], lower, ((1,), (1,)))
            beside = dot32(scaled, work_ref[at:after, after : after + BLOCK])
            current = work_ref[after : after + BLOCK, after : after + BLOCK] - dot32(below, beside)
        inverse = halves(dot32(lower, scaled, ((0,), (0,))))
        if not last:
            panel = dot_halves(inverse, halves(work_ref[at:after, after:]))
            panel_parts = halves(panel)
        turned = dot_halves(halves(out_ref[:, at:after]), inverse)
        turned_parts = halves(turned)
        for i in range(blocks):
            if i == p:
                continue
            span = slice(i * BLOCK, (i + 1) * BLOCK)
            column = halves(work_ref[span, at:after])
            if not last:
                work_ref[span, after:] -= dot_halves(column, panel_parts)
            out_ref[:, span] -= dot_halves(turned_parts, column, ((1,), (1,)))
        if not last:
            work_ref[at:after, after:] = panel
        out_ref[:, at:after] = turned


def diagonal_mask(count, nodes, first):
    row_at = lax.broadcasted_iota(jnp.int32, (count, nodes), 0) + first
    return row_at == lax.broadcasted_iota(jnp.int32, (count, nodes), 1)


def to_row(column, mask):
    return jnp.sum(jnp.where(mask, column, 0.0), axis=0, keepdims=True)


def write_packed(ref, start, rows, mask, vectors):
    count, nodes = rows.shape
    high = rows.astype(jnp.bfloat16)
    ref[start : start + count, :] = high
    lines = [to_row(rows - high.astype(jnp.float32), mask)]
    for vector in vectors:
        for _ in range(3):
            part = vector.astype(jnp.bfloat16).astype(jnp.float32)
            lines.append(part)
            vector = vector - part
    place = lax.broadcasted_iota(jnp.int32, (SPARE, nodes), 0)
    spare = jnp.zeros((SPARE, nodes), jnp.float32)
    for at, line in enumerate(lines):
        spare = jnp.where(place == at, jnp.broadcast_to(line, spare.shape), spare)
    ref[start + count : start + count + SPARE, :] = spare.astype(jnp.bfloat16)


def read_spare(ref, start, count):
    return ref[start + count : start + count + SPARE, :].astype(jnp.float32)


def spare_vector(spare, at):
    first = 1 + 3 * at
    return spare[first : first + 1] + (
        spare[first + 1 : first + 2] + spare[first + 2 : first + 3]
    )


def read_rows(ref, start, count, mask):
    rows = ref[start : start + count, :].astype(jnp.float32)
    return rows + jnp.where(mask, read_spare(ref, start, count)[0:1], 0.0)


def partner_product(solved, partner_ref, rest):
    high, low = halves(solved)

    def one(part):
        return lax.dot_general(
            part, partner_ref[...], (((1,), (1,)), ((), ())), preferred_element_type=jnp.float32
        )

    return one(high) + one(low) + solved * rest


def pack_kernel(cells_ref, rows_ref, coef_ref, prior_ref, out_ref):
    count, nodes = rows_ref.shape
    mask = diagonal_mask(count, nodes, cells_ref[0] * count)
    lane = lax.broadcasted_iota(jnp.int32, (1, nodes), 1)
    coef = jnp.where(lane == 0, jnp.broadcast_to(coef_ref[...], (1, nodes)), 0.0)
    prior = dot32(jnp.broadcast_to(prior_ref[...], (8, count)), mask.astype(jnp.float32))[0:1]
    write_packed(out_ref, 0, rows_ref[...], mask, (coef, prior))


def first_kernel(n_cells, cells_ref, coef_ref, prec_ref, gram_ref, *refs):
    own_refs, next_refs = refs[:n_cells], refs[n_cells : 2 * n_cells]
    sent_refs, fill_ref, diag_ref, rhs_ref = refs[2 * n_cells : 2 * n_cells + 4], *refs[
        2 * n_cells + 4 : 2 * n_cells + 7
    ]
    work_ref, out_ref, own_all, next_all, lower_ref, scaled_ref, ones_ref = refs[
        2 * n_cells + 7 :
    ]
    count, nodes = prec_ref.shape
    own_coef = coef_ref[...]
    next_spare = read_spare(next_refs[0], 0, count)
    next_coef = spare_vector(next_spare, 0)[:, 0:1]
    square = next_coef * next_coef
    own_rest = jnp.zeros((1, nodes), jnp.float32)
    next_rest = jnp.zeros((1, nodes), jnp.float32)
    rhs = gram_ref[nodes : nodes + 1, :] + gram_ref[nodes + 1 : nodes + 2, :]
    for k in range(n_cells):
        first = pl.multiple_of(cells_ref[k] * count, SPARE)
        span = pl.ds(first, count)
        mask = diagonal_mask(count, nodes, first)
        own_spare = read_spare(own_refs[k], 0, count)
        own_rest = own_rest + own_spare[0:1]
        next_rest = next_rest + read_spare(next_refs[k], 0, count)[0:1]
        prior = spare_vector(own_spare, 1)
        rhs = rhs + prior
        own_high, next_high = own_refs[k][0:count, :], next_refs[k][0:count, :]
        own_all[span, :] = own_high
        next_all[span, :] = next_high
        own_rows = read_rows(own_refs[k], 0, count, mask)
        next_rows = read_rows(next_refs[k], 0, count, mask)
        if k == 0:
            own_rows = prec_ref[...]
        rows = own_rows + square * next_rows + gram_ref[span, :]
        work_ref[span, :] = rows
        if k == 0:
            my_mask = mask
            diag_ref[...] = rows
            out_ref[0:count, :] = -own_coef * own_rows
            out_ref[count : 2 * count, :] = -next_coef * next_rows
    my_columns = jnp.sum(jnp.where(my_mask, 1.0, 0.0), axis=0, keepdims=True)
    rhs_ref[...] = jnp.broadcast_to(jnp.where(my_columns > 0.5, rhs, 0.0), rhs_ref.shape)
    gauss_jordan(work_ref, out_ref, lower_ref, scaled_ref, ones_ref)
    solved = out_ref[...]
    up = jnp.sum(solved * rhs, axis=1, keepdims=True)
    left = -own_coef * partner_product(solved, own_all, own_rest)
    right = -next_coef * partner_product(solved, next_all, next_rest)
    up_left, up_right = to_row(up[:count], my_mask), to_row(up[count:], my_mask)
    write_packed(sent_refs[0], 0, right[count:], my_mask, (up_right,))
    write_packed(sent_refs[1], 0, left[:count], my_mask, (up_left,))
    write_packed(sent_refs[2], 0, -right[:count], my_mask, ())
    write_packed(sent_refs[3], 0, -left[count:], my_mask, ())
    fill_ref[...] = -right[:count]


def merge_kernel(cells_ref, diag_ref, rhs_ref, left_ref, right_ref, pack_ref, out_ref, out_rhs):
    count, nodes = diag_ref.shape
    mask = diagonal_mask(count, nodes, cells_ref[0] * count)
    rows = (
        diag_ref[...] - read_rows(left_ref, 0, count, mask) - read_rows(right_ref, 0, count, mask)
    )
    rhs = (
        rhs_ref[0:1]
        - spare_vector(read_spare(left_ref, 0, count), 0)
        - spare_vector(read_spare(right_ref, 0, count), 0)
    )
    out_ref[...] = rows
    out_rhs[...] = jnp.broadcast_to(rhs, out_rhs.shape)
    write_packed(pack_ref, 0, rows, mask, (rhs,))


def second_kernel(n_cells, cells_ref, partner_ref, *refs):
    diag_refs = refs[:n_cells]
    out_ref, rhs_ref, work_ref, lower_ref, scaled_ref, ones_ref = refs[n_cells:]
    count = diag_refs[0].shape[0] - SPARE
    nodes = diag_refs[0].shape[1]
    size = count + SPARE
    rhs = jnp.zeros((1, nodes), jnp.float32)
    for k in range(n_cells):
        first = pl.multiple_of(cells_ref[k] * count, SPARE)
        mask = diagonal_mask(count, nodes, first)
        work_ref[pl.ds(first, count), :] = read_rows(diag_refs[k], 0, count, mask)
        rhs = rhs + spare_vector(read_spare(diag_refs[k], 0, count), 0)
        if k == 0:
            out_ref[0:count, :] = read_rows(partner_ref, 0, count, mask)
            out_ref[count : 2 * count, :] = read_rows(partner_ref, size, count, mask)
    rhs_ref[...] = jnp.broadcast_to(rhs, rhs_ref.shape)
    gauss_jordan(work_ref, out_ref, lower_ref, scaled_ref, ones_ref)


def last_kernel(n_cells, together, cells_ref, solved_ref, rhs_ref, *refs):
    pieces = refs[:n_cells]
    loss_ref, fill_ref, left_all, right_all = refs[n_cells:]
    nodes = solved_ref.shape[1]
    count = solved_ref.shape[0] // 2
    size = count + SPARE
    rests = [jnp.zeros((1, nodes), jnp.float32), jnp.zeros((1, nodes), jnp.float32)]
    for k in range(n_cells):
        span = pl.ds(pl.multiple_of(cells_ref[k] * count, SPARE), count)
        for side, target in enumerate((left_all, right_all)):
            start = side * size
            target[span, :] = pieces[k][start : start + count, :]
            rests[side] = rests[side] + read_spare(pieces[k], start, count)[0:1]
    mask = diagonal_mask(count, nodes, cells_ref[0] * count)
    solved = solved_ref[...]
    up = jnp.sum(solved * rhs_ref[0:1], axis=1, keepdims=True)
    up_left, up_right = to_row(up[:count], mask), to_row(up[count:], mask)
    left = partner_product(solved[:count], left_all, rests[0])
    right = partner_product(solved, right_all, rests[1])
    if together:
        write_packed(loss_ref, 0, left + right[count:], mask, (up_left + up_right,))
    else:
        write_packed(loss_ref, 0, left, mask, (up_left,))
        write_packed(loss_ref, size, right[count:], mask, (up_right,))
    fill_ref[...] = -right[:count]


def on_chip(kernel, name, out_shapes, scratch, operands, flops):
    vmem = pl.BlockSpec(memory_space=pltpu.VMEM)
    cells = pl.BlockSpec(memory_space=pltpu.SMEM)
    return pl.pallas_call(
        kernel,
        out_shape=[jax.ShapeDtypeStruct(shape, dtype) for shape, dtype in out_shapes],
        in_specs=[cells] + [vmem] * (len(operands) - 1),
        out_specs=[vmem] * len(out_shapes),
        scratch_shapes=[pltpu.VMEM(shape, dtype) for shape, dtype in scratch],
        cost_estimate=pl.CostEstimate(flops=flops, bytes_accessed=1 << 20, transcendentals=0),
        name=name,
    )(*operands)


def solve_scratch():
    return [
        ((2, BLOCK, BLOCK), jnp.float32),
        ((2, BLOCK, BLOCK), jnp.float32),
        ((PANEL, BLOCK), jnp.float32),
    ]


def shift(value, axis, steps, sources=None):
    count = lax.axis_size(axis)
    pairs = [
        (source, (source + steps) % count)
        for source in range(count)
        if sources is None or sources(source)
    ]
    return lax.ppermute(value, axis, pairs)


def cell_shifts():
    n_space, n_obs = lax.axis_size("space"), lax.axis_size("obs")
    return [(d, e) for e in range(n_obs) for d in range(n_space)]


def cell_table():
    n_space, n_obs = lax.axis_size("space"), lax.axis_size("obs")
    my_space, my_obs = lax.axis_index("space"), lax.axis_index("obs")
    cells = [
        lax.rem(my_space - d + n_space, n_space) * n_obs + lax.rem(my_obs - e + n_obs, n_obs)
        for d, e in cell_shifts()
    ]
    return jnp.stack(cells).astype(jnp.int32)


def spread(value):
    n_space, n_obs = lax.axis_size("space"), lax.axis_size("obs")
    along = [value] + [shift(value, "space", d) for d in range(1, n_space)]
    pieces = list(along)
    for e in range(1, n_obs):
        pieces += [shift(part, "obs", e) for part in along]
    return pieces


def spread_at_once(value):
    n_space, n_obs = lax.axis_size("space"), lax.axis_size("obs")
    pieces = []
    for d, e in cell_shifts()[1:]:
        pairs = [
            (s * n_obs + o, ((s + d) % n_space) * n_obs + (o + e) % n_obs)
            for s in range(n_space)
            for o in range(n_obs)
        ]
        pieces.append(lax.ppermute(value, GROUP, pairs))
    return pieces


def rounded(value):
    return lax.reduce_precision(value, 8, 7)


def unpack_rows(packed, mask):
    count = packed.shape[0] - SPARE
    rows = packed[:count].astype(jnp.float32)
    return rows + jnp.where(mask, packed[count].astype(jnp.float32)[None, :], 0.0)


def unpack_vector(packed):
    first = packed.shape[0] - SPARE + 1
    parts = packed[first : first + 3].astype(jnp.float32)
    return parts[0] + (parts[1] + parts[2])


def routed_rows(obs_panel, node_index, weight, residual, route_time, n_times):
    rows_dev, nodes = obs_panel.shape
    capacity = 2 * rows_dev // n_times
    root = jnp.sqrt(weight.astype(jnp.float32))
    node_hits = node_index[:, None] == lax.iota(jnp.int32, nodes)[None, :]
    design = rounded(obs_panel.astype(jnp.float32) + node_hits.astype(jnp.float32))
    scaled = (root[:, None] * design).astype(jnp.bfloat16)
    target = root * residual.astype(jnp.float32)
    target_high = rounded(target)
    same = route_time[:, None] == route_time[None, :]
    earlier = lax.iota(jnp.int32, rows_dev)[:, None] > lax.iota(jnp.int32, rows_dev)[None, :]
    rank = jnp.sum((same & earlier).astype(jnp.int32), axis=1)
    ahead = lax.rem(route_time - lax.axis_index("tm") + n_times, n_times)
    column = lax.iota(jnp.int32, SPARE)[None, :]
    extra = jnp.where(
        column == 0,
        target_high[:, None],
        jnp.where(column == 1, (target - target_high)[:, None], 0.0),
    ).astype(jnp.bfloat16)
    rows = jnp.concatenate([scaled, extra], axis=1)
    slots = lax.iota(jnp.int32, capacity)[None, :]
    parts = []
    for step in range(n_times):
        slot_of = (ahead[:, None] == step) & (rank[:, None] == slots)
        part = lax.dot_general(
            rows,
            slot_of.astype(jnp.bfloat16),
            (((0,), (0,)), ((), ())),
            preferred_element_type=jnp.float32,
        ).astype(jnp.bfloat16)
        parts.append(shift(part, "tm", step) if step else part)
    return parts


def moments(slots, nodes):
    return lax.dot_general(
        slots, slots[:nodes], (((1,), (1,)), ((), ())), preferred_element_type=jnp.float32
    )


def local(obs_panel, node_index, weight, residual, route_time, spatial_prec, ar_coef, prior_rhs):
    n_times = lax.axis_size("tm")
    n_space, n_obs = lax.axis_size("space"), lax.axis_size("obs")
    n_cells = n_space * n_obs
    time_index = lax.axis_index("tm")
    nodes = obs_panel.shape[1]
    count = spatial_prec.shape[1]
    size = count + SPARE
    assert nodes % BLOCK == 0 and count % SPARE == 0
    cells = cell_table()
    first_row = cells[0] * count
    own_prec, coef = spatial_prec[0], ar_coef.reshape(1, 1)
    (own_pack,) = on_chip(
        pack_kernel,
        "pack_prior",
        [((size, nodes), jnp.bfloat16)],
        [],
        (cells, own_prec, coef, prior_rhs),
        0,
    )
    own_pack, route_time = lax.optimization_barrier((own_pack, route_time))
    from_next = shift(own_pack, "tm", -1)
    own_pieces = spread(own_pack)
    parts = routed_rows(obs_panel, node_index, weight, residual, route_time, n_times)
    next_pieces = spread(from_next)
    parts[1:], own_pieces[:n_space], next_pieces[:n_space] = lax.optimization_barrier(
        (parts[1:], own_pieces[:n_space], next_pieces[:n_space])
    )

    arrived = jnp.concatenate(parts, axis=1)
    near = [arrived] + [shift(arrived, "obs", e) for e in range(1, n_obs)]
    far = [
        jnp.concatenate([shift(part, "space", d) for part in parts], axis=1)
        for d in range(1, n_space)
    ]
    far += [shift(part, "obs", e) for e in range(1, n_obs) for part in far]
    gram = moments(near[0], nodes)
    for part in near[1:] + far:
        gram = gram + moments(part, nodes)

    loss_right, loss_left, pack_fill, pack_turn, fill_one, diag_one, rhs_one = on_chip(
        functools.partial(first_kernel, n_cells),
        "level_one",
        [((size, nodes), jnp.bfloat16)] * 4
        + [
            ((count, nodes), jnp.float32),
            ((count, nodes), jnp.float32),
            ((8, nodes), jnp.float32),
        ],
        [
            ((nodes, nodes), jnp.float32),
            ((2 * count, nodes), jnp.float32),
            ((nodes, nodes), jnp.bfloat16),
            ((nodes, nodes), jnp.bfloat16),
        ]
        + solve_scratch(),
        (cells, coef, own_prec, gram, *own_pieces, *next_pieces),
        70 * nodes**3,
    )
    def is_second(time):
        return time % 4 == 2

    def after_one(time):
        return time % 4 == 1

    def before_none(time):
        return time % 4 == 3

    came_left = shift(loss_right, "tm", 1, after_one)
    came_right = shift(loss_left, "tm", -1, before_none)
    pack_fill, pack_turn, came_left, came_right = lax.optimization_barrier(
        (pack_fill, pack_turn, came_left, came_right)
    )
    fill_left = shift(pack_fill, "tm", 1, after_one)
    fill_right = shift(pack_turn, "tm", -1, before_none)

    pack_two, diag_two, rhs_two = on_chip(
        merge_kernel,
        "merge_losses",
        [
            ((size, nodes), jnp.bfloat16),
            ((count, nodes), jnp.float32),
            ((8, nodes), jnp.float32),
        ],
        [],
        (cells, diag_one, rhs_one, came_left, came_right),
        0,
    )
    pieces_two = spread(pack_two)
    fill_left, fill_right, pieces_two[0], loss_right, loss_left = lax.optimization_barrier(
        (fill_left, fill_right, pieces_two[0], loss_right, loss_left)
    )
    partner = jnp.concatenate([fill_left, fill_right], axis=0)
    partners = spread_at_once(partner)
    late_left = shift(loss_right, "tm", 1, before_none)
    late_right = shift(loss_left, "tm", -1, after_one)
    solved, rhs_full = on_chip(
        functools.partial(second_kernel, n_cells),
        "level_two",
        [((2 * count, nodes), jnp.float32), ((8, nodes), jnp.float32)],
        [((nodes, nodes), jnp.float32)] + solve_scratch(),
        (cells, partner, *pieces_two),
        60 * nodes**3,
    )
    together = 4 % n_times == 0
    loss_two, fill_two = on_chip(
        functools.partial(last_kernel, n_cells, together),
        "products_two",
        [
            ((size if together else 2 * size, nodes), jnp.bfloat16),
            ((count, nodes), jnp.float32),
        ],
        [((nodes, nodes), jnp.bfloat16), ((nodes, nodes), jnp.bfloat16)],
        (cells, solved, rhs_full, partner, *partners),
        4 * nodes**3,
    )

    if together:
        came = [shift(loss_two, "tm", 2, is_second)]
    else:
        came = [
            shift(loss_two[:size], "tm", -2, is_second),
            shift(loss_two[size:], "tm", 2, is_second),
        ]
    mask = diagonal_mask(count, nodes, first_row)
    diag_out = diag_two - unpack_rows(late_left, mask) - unpack_rows(late_right, mask)
    rhs_out = rhs_two[0] - unpack_vector(late_left) - unpack_vector(late_right)
    for part in came:
        diag_out = diag_out - unpack_rows(part, mask)
        rhs_out = rhs_out - unpack_vector(part)
    rhs_out = lax.dynamic_slice_in_dim(rhs_out, first_row, count, 0)
    fill_out = jnp.where(
        time_index % 2 == 1,
        fill_one,
        jnp.where(is_second(time_index), fill_two, jnp.zeros_like(fill_two)),
    )
    return (diag_out[None], fill_out[None], rhs_out[None])


def solution(mesh):
    return jax.shard_map(
        local,
        mesh=mesh,
        in_specs=(
            P(("grp", "tm", "space", "obs"), None),
            P(("grp", "tm", "space", "obs")),
            P(("grp", "tm", "space", "obs")),
            P(("grp", "tm", "space", "obs")),
            P(("grp", "tm", "space", "obs")),
            P(("grp", "tm"), ("space", "obs"), None),
            P(("grp", "tm")),
            P(("grp", "tm"), ("space", "obs")),
        ),
        out_specs=(
            P(("grp", "tm"), ("space", "obs"), None),
            P(("grp", "tm"), ("space", "obs"), None),
            P(("grp", "tm"), ("space", "obs")),
        ),
        check_vma=False,
    )
```

```python
import functools

import jax
import jax.numpy as jnp
from jax import lax
from jax.experimental import pallas as pl
from jax.experimental.pallas import tpu as pltpu
from jax.sharding import PartitionSpec as P


BLOCK = 128
PANEL = 8
HIGHEST = lax.Precision.HIGHEST


def across(value, lane_index):
    return jnp.broadcast_to(value[:, lane_index : lane_index + 1], value.shape)


def down(value, row_index):
    return jnp.broadcast_to(value[row_index : row_index + 1, :], value.shape)


def tree_sum(terms):
    terms = list(terms)
    while len(terms) > 1:
        terms = [
            terms[at] + terms[at + 1] if at + 1 < len(terms) else terms[at]
            for at in range(0, len(terms), 2)
        ]
    return terms[0]


def dot32(left, right, dims=((1,), (0,))):
    return lax.dot_general(
        left, right, (dims, ((), ())), precision=HIGHEST, preferred_element_type=jnp.float32
    )


def halves(value):
    high = value.astype(jnp.bfloat16)
    return high, (value - high.astype(jnp.float32)).astype(jnp.bfloat16)


def dot_halves(left, right, dims=((1,), (0,))):
    def one(a, b):
        return lax.dot_general(a, b, (dims, ((), ())), preferred_element_type=jnp.float32)

    return one(left[0], right[0]) + (one(left[0], right[1]) + one(left[1], right[0]))


def panel_step(panel, first, lane, sub, ones):
    cols = [across(panel, first + j) * ones for j in range(PANEL)]
    entry = [[None] * PANEL for _ in range(PANEL)]
    for i in range(PANEL):
        for j in range(i, PANEL):
            entry[i][j] = entry[j][i] = down(cols[j], i)
    inside = (lane >= first) & (lane < first + PANEL)
    augmented = jnp.where(inside, jnp.where(lane == first + sub, 1.0, 0.0), panel)
    lower = jnp.where(lane < first + PANEL, augmented, 0.0)
    rows = [down(augmented, i) for i in range(PANEL)]
    for j in range(0, PANEL, 2):
        p, b, s = entry[j][j], entry[j][j + 1], entry[j + 1][j + 1]
        r = 1.0 / (p * s - b * b)
        upper_new, lower_new = {}, {}
        for m in range(j + 2, PANEL):
            upper_new[m] = (s * entry[j][m] - b * entry[j + 1][m]) * r
            lower_new[m] = (p * entry[j + 1][m] - b * entry[j][m]) * r
        upper_row = (s * rows[j] - b * rows[j + 1]) * r
        lower_row = (p * rows[j + 1] - b * rows[j]) * r
        for i in range(PANEL):
            if i in (j, j + 1):
                continue
            f, g = entry[i][j], entry[i][j + 1]
            for m in range(max(j + 2, i if i > j else 0), PANEL):
                value = entry[i][m] - (f * upper_new[m] + g * lower_new[m])
                entry[i][m] = value
                if i > j and m > i:
                    entry[m][i] = value
            rows[i] = rows[i] - (f * upper_row + g * lower_row)
        for m in range(j + 2, PANEL):
            entry[j][m] = upper_new[m]
            entry[j + 1][m] = lower_new[m]
        rows[j], rows[j + 1] = upper_row, lower_row
    solved = rows[0]
    for i in range(1, PANEL):
        solved = jnp.where(sub == i, rows[i], solved)
    return lower, rows, solved, inside


def factor_block(block, lower_ref, scaled_ref, ones):
    count = BLOCK // PANEL
    lane = lax.broadcasted_iota(jnp.int32, (PANEL, BLOCK), 1)
    sub = lax.broadcasted_iota(jnp.int32, (PANEL, BLOCK), 0)
    rows = [block[PANEL * i : PANEL * (i + 1), :] for i in range(count)]
    for q in range(count):
        first = q * PANEL
        lower, pivot_rows, solved, inside = panel_step(rows[q], first, lane, sub, ones)
        lower_ref[first : first + PANEL, :] = lower
        scaled_ref[first : first + PANEL, :] = jnp.where(lane < first + PANEL, solved, 0.0)
        for i in range(q + 1, count):
            change = tree_sum(
                across(rows[i], first + j) * pivot_rows[j] for j in range(PANEL)
            )
            rows[i] = jnp.where(inside, 0.0, rows[i]) - change


SPARE = 16
GROUP = ("space", "obs")


def gauss_jordan(work_ref, out_ref, lower_ref, scaled_ref, ones_ref):
    blocks = work_ref.shape[0] // BLOCK
    ones_ref[...] = jnp.ones_like(ones_ref)
    ones = ones_ref[...]
    current = work_ref[0:BLOCK, 0:BLOCK]
    for p in range(blocks):
        at, after = p * BLOCK, (p + 1) * BLOCK
        last = p == blocks - 1
        slot = p % 2
        factor_block(current, lower_ref.at[slot], scaled_ref.at[slot], ones)
        lower, scaled = lower_ref[slot], scaled_ref[slot]
        lower, scaled = halves(lower), halves(scaled)
        if not last:
            below = dot_halves(
                halves(work_ref[after : after + BLOCK, at:after]), lower, ((1,), (1,))
            )
            beside = dot_halves(scaled, halves(work_ref[at:after, after : after + BLOCK]))
            current = work_ref[after : after + BLOCK, after : after + BLOCK] - dot_halves(
                halves(below), halves(beside)
            )
        inverse = halves(dot_halves(lower, scaled, ((0,), (0,))))
        if not last:
            panel = dot_halves(inverse, halves(work_ref[at:after, after:]))
            panel_parts = halves(panel)
        turned = dot_halves(halves(out_ref[:, at:after]), inverse)
        turned_parts = halves(turned)
        for i in range(blocks):
            if i == p:
                continue
            span = slice(i * BLOCK, (i + 1) * BLOCK)
            column = halves(work_ref[span, at:after])
            if not last:
                work_ref[span, after:] -= dot_halves(column, panel_parts)
            out_ref[:, span] -= dot_halves(turned_parts, column, ((1,), (1,)))
        if not last:
            work_ref[at:after, after:] = panel
        out_ref[:, at:after] = turned


def diagonal_mask(count, nodes, first):
    row_at = lax.broadcasted_iota(jnp.int32, (count, nodes), 0) + first
    return row_at == lax.broadcasted_iota(jnp.int32, (count, nodes), 1)


def to_row(column, mask):
    return jnp.sum(jnp.where(mask, column, 0.0), axis=0, keepdims=True)


def write_packed(ref, start, rows, mask, vectors):
    count, nodes = rows.shape
    high = rows.astype(jnp.bfloat16)
    ref[start : start + count, :] = high
    lines = [to_row(rows - high.astype(jnp.float32), mask)]
    for vector in vectors:
        for _ in range(3):
            part = vector.astype(jnp.bfloat16).astype(jnp.float32)
            lines.append(part)
            vector = vector - part
    place = lax.broadcasted_iota(jnp.int32, (SPARE, nodes), 0)
    spare = jnp.zeros((SPARE, nodes), jnp.float32)
    for at, line in enumerate(lines):
        spare = jnp.where(place == at, jnp.broadcast_to(line, spare.shape), spare)
    ref[start + count : start + count + SPARE, :] = spare.astype(jnp.bfloat16)


def read_spare(ref, start, count):
    return ref[start + count : start + count + SPARE, :].astype(jnp.float32)


def spare_vector(spare, at):
    first = 1 + 3 * at
    return spare[first : first + 1] + (
        spare[first + 1 : first + 2] + spare[first + 2 : first + 3]
    )


def read_rows(ref, start, count, mask):
    rows = ref[start : start + count, :].astype(jnp.float32)
    return rows + jnp.where(mask, read_spare(ref, start, count)[0:1], 0.0)


def partner_product(solved, partner_ref, rest):
    high, low = halves(solved)

    def one(part):
        return lax.dot_general(
            part, partner_ref[...], (((1,), (1,)), ((), ())), preferred_element_type=jnp.float32
        )

    return one(high) + one(low) + solved * rest


def pack_kernel(cells_ref, rows_ref, coef_ref, prior_ref, out_ref):
    count, nodes = rows_ref.shape
    mask = diagonal_mask(count, nodes, cells_ref[0] * count)
    lane = lax.broadcasted_iota(jnp.int32, (1, nodes), 1)
    coef = jnp.where(lane == 0, jnp.broadcast_to(coef_ref[...], (1, nodes)), 0.0)
    prior = dot32(jnp.broadcast_to(prior_ref[...], (8, count)), mask.astype(jnp.float32))[0:1]
    write_packed(out_ref, 0, rows_ref[...], mask, (coef, prior))


def rows_kernel(n_times, at_ref, panel_ref, node_ref, weight_ref, residual_ref, time_ref, *refs):
    rows_ref, mark_refs = refs[0], refs[1:]
    count, nodes = panel_ref.shape
    capacity = mark_refs[0].shape[1]
    line = lax.broadcasted_iota(jnp.int32, (8, count), 0)
    lines = jnp.zeros((8, count), jnp.float32)
    time_row = time_ref[...].astype(jnp.float32)
    for at, value in enumerate((time_row, node_ref[...], weight_ref[...], residual_ref[...])):
        lines = jnp.where(line == at, value.astype(jnp.float32), lines)
    columns = lines.T
    time, node, weight, residual = (columns[:, at : at + 1] for at in range(4))
    root = jnp.sqrt(weight)
    lane = lax.broadcasted_iota(jnp.int32, (count, nodes), 1).astype(jnp.float32)
    design = panel_ref[...].astype(jnp.float32) + jnp.where(lane == node, 1.0, 0.0)
    design = design.astype(jnp.bfloat16).astype(jnp.float32)
    rows_ref[:, 0:nodes] = (root * design).astype(jnp.bfloat16)
    target = root * residual
    high = target.astype(jnp.bfloat16).astype(jnp.float32)
    place = lax.broadcasted_iota(jnp.int32, (count, SPARE), 1)
    extra = jnp.where(place == 0, high, jnp.where(place == 1, target - high, 0.0))
    rows_ref[:, nodes : nodes + SPARE] = extra.astype(jnp.bfloat16)
    earlier = lax.broadcasted_iota(jnp.int32, (count, count), 1) < lax.broadcasted_iota(
        jnp.int32, (count, count), 0
    )
    rank = jnp.sum(
        jnp.where((time == time_row) & earlier, 1.0, 0.0), axis=1, keepdims=True
    )
    ahead = time - at_ref[0].astype(jnp.float32)
    ahead = jnp.where(ahead < 0.0, ahead + n_times, ahead)
    slot = lax.broadcasted_iota(jnp.int32, (count, capacity), 1).astype(jnp.float32)
    for step in range(n_times):
        mark_refs[step][...] = jnp.where((ahead == step) & (rank == slot), 1.0, 0.0).astype(
            jnp.bfloat16
        )


def first_kernel(n_cells, cells_ref, coef_ref, prec_ref, gram_ref, *refs):
    own_refs, next_refs = refs[:n_cells], refs[n_cells : 2 * n_cells]
    sent_refs, fill_ref, diag_ref, rhs_ref = refs[2 * n_cells : 2 * n_cells + 4], *refs[
        2 * n_cells + 4 : 2 * n_cells + 7
    ]
    work_ref, out_ref, own_all, next_all, lower_ref, scaled_ref, ones_ref = refs[
        2 * n_cells + 7 :
    ]
    count, nodes = prec_ref.shape
    own_coef = coef_ref[...]
    next_spare = read_spare(next_refs[0], 0, count)
    next_coef = spare_vector(next_spare, 0)[:, 0:1]
    square = next_coef * next_coef
    own_rest = jnp.zeros((1, nodes), jnp.float32)
    next_rest = jnp.zeros((1, nodes), jnp.float32)
    rhs = gram_ref[nodes : nodes + 1, :] + gram_ref[nodes + 1 : nodes + 2, :]
    for k in range(n_cells):
        first = pl.multiple_of(cells_ref[k] * count, SPARE)
        span = pl.ds(first, count)
        mask = diagonal_mask(count, nodes, first)
        own_spare = read_spare(own_refs[k], 0, count)
        own_rest = own_rest + own_spare[0:1]
        next_rest = next_rest + read_spare(next_refs[k], 0, count)[0:1]
        prior = spare_vector(own_spare, 1)
        rhs = rhs + prior
        own_high, next_high = own_refs[k][0:count, :], next_refs[k][0:count, :]
        own_all[span, :] = own_high
        next_all[span, :] = next_high
        own_rows = read_rows(own_refs[k], 0, count, mask)
        next_rows = read_rows(next_refs[k], 0, count, mask)
        if k == 0:
            own_rows = prec_ref[...]
        rows = own_rows + square * next_rows + gram_ref[span, :]
        work_ref[span, :] = rows
        if k == 0:
            my_mask = mask
            diag_ref[...] = rows
            out_ref[0:count, :] = -own_coef * own_rows
            out_ref[count : 2 * count, :] = -next_coef * next_rows
    my_columns = jnp.sum(jnp.where(my_mask, 1.0, 0.0), axis=0, keepdims=True)
    rhs_ref[...] = jnp.broadcast_to(jnp.where(my_columns > 0.5, rhs, 0.0), rhs_ref.shape)
    gauss_jordan(work_ref, out_ref, lower_ref, scaled_ref, ones_ref)
    solved = out_ref[...]
    up = jnp.sum(solved * rhs, axis=1, keepdims=True)
    left = -own_coef * partner_product(solved, own_all, own_rest)
    right = -next_coef * partner_product(solved, next_all, next_rest)
    up_left, up_right = to_row(up[:count], my_mask), to_row(up[count:], my_mask)
    write_packed(sent_refs[0], 0, right[count:], my_mask, (up_right,))
    write_packed(sent_refs[1], 0, left[:count], my_mask, (up_left,))
    write_packed(sent_refs[2], 0, -right[:count], my_mask, ())
    write_packed(sent_refs[3], 0, -left[count:], my_mask, ())
    fill_ref[...] = -right[:count]


def merge_kernel(cells_ref, diag_ref, rhs_ref, left_ref, right_ref, pack_ref, out_ref, out_rhs):
    count, nodes = diag_ref.shape
    mask = diagonal_mask(count, nodes, cells_ref[0] * count)
    rows = (
        diag_ref[...] - read_rows(left_ref, 0, count, mask) - read_rows(right_ref, 0, count, mask)
    )
    rhs = (
        rhs_ref[0:1]
        - spare_vector(read_spare(left_ref, 0, count), 0)
        - spare_vector(read_spare(right_ref, 0, count), 0)
    )
    out_ref[...] = rows
    out_rhs[...] = jnp.broadcast_to(rhs, out_rhs.shape)
    write_packed(pack_ref, 0, rows, mask, (rhs,))


def second_kernel(n_cells, cells_ref, partner_ref, *refs):
    diag_refs = refs[:n_cells]
    out_ref, rhs_ref, work_ref, lower_ref, scaled_ref, ones_ref = refs[n_cells:]
    count = diag_refs[0].shape[0] - SPARE
    nodes = diag_refs[0].shape[1]
    size = count + SPARE
    rhs = jnp.zeros((1, nodes), jnp.float32)
    for k in range(n_cells):
        first = pl.multiple_of(cells_ref[k] * count, SPARE)
        mask = diagonal_mask(count, nodes, first)
        work_ref[pl.ds(first, count), :] = read_rows(diag_refs[k], 0, count, mask)
        rhs = rhs + spare_vector(read_spare(diag_refs[k], 0, count), 0)
        if k == 0:
            out_ref[0:count, :] = read_rows(partner_ref, 0, count, mask)
            out_ref[count : 2 * count, :] = read_rows(partner_ref, size, count, mask)
    rhs_ref[...] = jnp.broadcast_to(rhs, rhs_ref.shape)
    gauss_jordan(work_ref, out_ref, lower_ref, scaled_ref, ones_ref)


def last_kernel(n_cells, together, cells_ref, solved_ref, rhs_ref, *refs):
    pieces = refs[:n_cells]
    loss_ref, fill_ref, left_all, right_all = refs[n_cells:]
    nodes = solved_ref.shape[1]
    count = solved_ref.shape[0] // 2
    size = count + SPARE
    rests = [jnp.zeros((1, nodes), jnp.float32), jnp.zeros((1, nodes), jnp.float32)]
    for k in range(n_cells):
        span = pl.ds(pl.multiple_of(cells_ref[k] * count, SPARE), count)
        for side, target in enumerate((left_all, right_all)):
            start = side * size
            target[span, :] = pieces[k][start : start + count, :]
            rests[side] = rests[side] + read_spare(pieces[k], start, count)[0:1]
    mask = diagonal_mask(count, nodes, cells_ref[0] * count)
    solved = solved_ref[...]
    up = jnp.sum(solved * rhs_ref[0:1], axis=1, keepdims=True)
    up_left, up_right = to_row(up[:count], mask), to_row(up[count:], mask)
    left = partner_product(solved[:count], left_all, rests[0])
    right = partner_product(solved, right_all, rests[1])
    if together:
        write_packed(loss_ref, 0, left + right[count:], mask, (up_left + up_right,))
    else:
        write_packed(loss_ref, 0, left, mask, (up_left,))
        write_packed(loss_ref, size, right[count:], mask, (up_right,))
    fill_ref[...] = -right[:count]


def on_chip(kernel, name, out_shapes, scratch, operands, flops):
    vmem = pl.BlockSpec(memory_space=pltpu.VMEM)
    cells = pl.BlockSpec(memory_space=pltpu.SMEM)
    return pl.pallas_call(
        kernel,
        out_shape=[jax.ShapeDtypeStruct(shape, dtype) for shape, dtype in out_shapes],
        in_specs=[cells] + [vmem] * (len(operands) - 1),
        out_specs=[vmem] * len(out_shapes),
        scratch_shapes=[pltpu.VMEM(shape, dtype) for shape, dtype in scratch],
        cost_estimate=pl.CostEstimate(flops=flops, bytes_accessed=1 << 20, transcendentals=0),
        name=name,
    )(*operands)


def solve_scratch():
    return [
        ((2, BLOCK, BLOCK), jnp.float32),
        ((2, BLOCK, BLOCK), jnp.float32),
        ((PANEL, BLOCK), jnp.float32),
    ]


def shift(value, axis, steps, sources=None):
    count = lax.axis_size(axis)
    pairs = [
        (source, (source + steps) % count)
        for source in range(count)
        if sources is None or sources(source)
    ]
    return lax.ppermute(value, axis, pairs)


def cell_shifts():
    n_space, n_obs = lax.axis_size("space"), lax.axis_size("obs")
    return [(d, e) for e in range(n_obs) for d in range(n_space)]


def cell_table():
    n_space, n_obs = lax.axis_size("space"), lax.axis_size("obs")
    my_space, my_obs = lax.axis_index("space"), lax.axis_index("obs")
    cells = [
        lax.rem(my_space - d + n_space, n_space) * n_obs + lax.rem(my_obs - e + n_obs, n_obs)
        for d, e in cell_shifts()
    ]
    return jnp.stack(cells).astype(jnp.int32)


def spread(value):
    n_space, n_obs = lax.axis_size("space"), lax.axis_size("obs")
    along = [value] + [shift(value, "space", d) for d in range(1, n_space)]
    pieces = list(along)
    for e in range(1, n_obs):
        pieces += [shift(part, "obs", e) for part in along]
    return pieces


def spread_at_once(value):
    n_space, n_obs = lax.axis_size("space"), lax.axis_size("obs")
    pieces = []
    for d, e in cell_shifts()[1:]:
        pairs = [
            (s * n_obs + o, ((s + d) % n_space) * n_obs + (o + e) % n_obs)
            for s in range(n_space)
            for o in range(n_obs)
        ]
        pieces.append(lax.ppermute(value, GROUP, pairs))
    return pieces


def unpack_rows(packed, mask):
    count = packed.shape[0] - SPARE
    rows = packed[:count].astype(jnp.float32)
    return rows + jnp.where(mask, packed[count].astype(jnp.float32)[None, :], 0.0)


def unpack_vector(packed):
    first = packed.shape[0] - SPARE + 1
    parts = packed[first : first + 3].astype(jnp.float32)
    return parts[0] + (parts[1] + parts[2])


def routed_rows(obs_panel, node_index, weight, residual, route_time, n_times):
    rows_dev, nodes = obs_panel.shape
    capacity = 2 * rows_dev // n_times
    rows, *marks = on_chip(
        functools.partial(rows_kernel, n_times),
        "scale_rows",
        [((rows_dev, nodes + SPARE), jnp.bfloat16)]
        + [((rows_dev, capacity), jnp.bfloat16)] * n_times,
        [],
        (
            lax.axis_index("tm").astype(jnp.int32).reshape(1),
            obs_panel,
            node_index.reshape(1, rows_dev),
            weight.reshape(1, rows_dev),
            residual.reshape(1, rows_dev),
            route_time.reshape(1, rows_dev),
        ),
        0,
    )
    parts = []
    for step, mark in enumerate(marks):
        part = lax.dot_general(
            rows,
            mark,
            (((0,), (0,)), ((), ())),
            preferred_element_type=jnp.float32,
        ).astype(jnp.bfloat16)
        parts.append(shift(part, "tm", step) if step else part)
    return parts


def moments(slots, nodes):
    return lax.dot_general(
        slots, slots[:nodes], (((1,), (1,)), ((), ())), preferred_element_type=jnp.float32
    )


def local(obs_panel, node_index, weight, residual, route_time, spatial_prec, ar_coef, prior_rhs):
    n_times = lax.axis_size("tm")
    n_space, n_obs = lax.axis_size("space"), lax.axis_size("obs")
    n_cells = n_space * n_obs
    time_index = lax.axis_index("tm")
    nodes = obs_panel.shape[1]
    count = spatial_prec.shape[1]
    size = count + SPARE
    assert nodes % BLOCK == 0 and count % SPARE == 0
    cells = cell_table()
    first_row = cells[0] * count
    own_prec, coef = spatial_prec[0], ar_coef.reshape(1, 1)
    (own_pack,) = on_chip(
        pack_kernel,
        "pack_prior",
        [((size, nodes), jnp.bfloat16)],
        [],
        (cells, own_prec, coef, prior_rhs),
        0,
    )
    own_pack, route_time = lax.optimization_barrier((own_pack, route_time))
    from_next = shift(own_pack, "tm", -1)
    own_pieces = spread(own_pack)
    parts = routed_rows(obs_panel, node_index, weight, residual, route_time, n_times)
    next_pieces = spread(from_next)
    own_slots = [shift(parts[0], "space", d) for d in range(1, n_space)]
    parts[1:], own_pieces[:n_space], next_pieces[:n_space], own_slots = lax.optimization_barrier(
        (parts[1:], own_pieces[:n_space], next_pieces[:n_space], own_slots)
    )

    arrived = jnp.concatenate(parts, axis=1)
    near = [arrived] + [shift(arrived, "obs", e) for e in range(1, n_obs)]
    gram = sum(moments(part, nodes) for part in near)
    for d in range(1, n_space):
        slots = [own_slots[d - 1]] + [shift(part, "space", d) for part in parts[1:]]
        slots, gram = lax.optimization_barrier((slots, gram))
        far = jnp.concatenate(slots, axis=1)
        gram = gram + moments(far, nodes)
        for e in range(1, n_obs):
            gram = gram + moments(shift(far, "obs", e), nodes)

    loss_right, loss_left, pack_fill, pack_turn, fill_one, diag_one, rhs_one = on_chip(
        functools.partial(first_kernel, n_cells),
        "level_one",
        [((size, nodes), jnp.bfloat16)] * 4
        + [
            ((count, nodes), jnp.float32),
            ((count, nodes), jnp.float32),
            ((8, nodes), jnp.float32),
        ],
        [
            ((nodes, nodes), jnp.float32),
            ((2 * count, nodes), jnp.float32),
            ((nodes, nodes), jnp.bfloat16),
            ((nodes, nodes), jnp.bfloat16),
        ]
        + solve_scratch(),
        (cells, coef, own_prec, gram, *own_pieces, *next_pieces),
        70 * nodes**3,
    )
    def is_second(time):
        return time % 4 == 2

    def after_one(time):
        return time % 4 == 1

    def before_none(time):
        return time % 4 == 3

    came_left = shift(loss_right, "tm", 1, after_one)
    came_right = shift(loss_left, "tm", -1, before_none)
    pack_fill, pack_turn, came_left, came_right = lax.optimization_barrier(
        (pack_fill, pack_turn, came_left, came_right)
    )
    fill_left = shift(pack_fill, "tm", 1, after_one)
    fill_right = shift(pack_turn, "tm", -1, before_none)

    pack_two, diag_two, rhs_two = on_chip(
        merge_kernel,
        "merge_losses",
        [
            ((size, nodes), jnp.bfloat16),
            ((count, nodes), jnp.float32),
            ((8, nodes), jnp.float32),
        ],
        [],
        (cells, diag_one, rhs_one, came_left, came_right),
        0,
    )
    pieces_two = spread(pack_two)
    fill_left, fill_right, pieces_two[0], loss_right, loss_left = lax.optimization_barrier(
        (fill_left, fill_right, pieces_two[0], loss_right, loss_left)
    )
    partner = jnp.concatenate([fill_left, fill_right], axis=0)
    partners = spread_at_once(partner)
    late_left = shift(loss_right, "tm", 1, before_none)
    late_right = shift(loss_left, "tm", -1, after_one)
    solved, rhs_full = on_chip(
        functools.partial(second_kernel, n_cells),
        "level_two",
        [((2 * count, nodes), jnp.float32), ((8, nodes), jnp.float32)],
        [((nodes, nodes), jnp.float32)] + solve_scratch(),
        (cells, partner, *pieces_two),
        60 * nodes**3,
    )
    together = 4 % n_times == 0
    loss_two, fill_two = on_chip(
        functools.partial(last_kernel, n_cells, together),
        "products_two",
        [
            ((size if together else 2 * size, nodes), jnp.bfloat16),
            ((count, nodes), jnp.float32),
        ],
        [((nodes, nodes), jnp.bfloat16), ((nodes, nodes), jnp.bfloat16)],
        (cells, solved, rhs_full, partner, *partners),
        4 * nodes**3,
    )

    if together:
        came = [shift(loss_two, "tm", 2, is_second)]
    else:
        came = [
            shift(loss_two[:size], "tm", -2, is_second),
            shift(loss_two[size:], "tm", 2, is_second),
        ]
    mask = diagonal_mask(count, nodes, first_row)
    diag_out = diag_two - unpack_rows(late_left, mask) - unpack_rows(late_right, mask)
    rhs_out = rhs_two[0] - unpack_vector(late_left) - unpack_vector(late_right)
    for part in came:
        diag_out = diag_out - unpack_rows(part, mask)
        rhs_out = rhs_out - unpack_vector(part)
    rhs_out = lax.dynamic_slice_in_dim(rhs_out, first_row, count, 0)
    fill_out = jnp.where(
        time_index % 2 == 1,
        fill_one,
        jnp.where(is_second(time_index), fill_two, jnp.zeros_like(fill_two)),
    )
    return (diag_out[None], fill_out[None], rhs_out[None])


def solution(mesh):
    return jax.shard_map(
        local,
        mesh=mesh,
        in_specs=(
            P(("grp", "tm", "space", "obs"), None),
            P(("grp", "tm", "space", "obs")),
            P(("grp", "tm", "space", "obs")),
            P(("grp", "tm", "space", "obs")),
            P(("grp", "tm", "space", "obs")),
            P(("grp", "tm"), ("space", "obs"), None),
            P(("grp", "tm")),
            P(("grp", "tm"), ("space", "obs")),
        ),
        out_specs=(
            P(("grp", "tm"), ("space", "obs"), None),
            P(("grp", "tm"), ("space", "obs"), None),
            P(("grp", "tm"), ("space", "obs")),
        ),
        check_vma=False,
    )
```

```python
import functools

import jax
import jax.numpy as jnp
from jax import lax
from jax.experimental import pallas as pl
from jax.experimental.pallas import tpu as pltpu
from jax.sharding import PartitionSpec as P


BLOCK = 128
PANEL = 8
HIGHEST = lax.Precision.HIGHEST


def across(value, lane_index):
    return jnp.broadcast_to(value[:, lane_index : lane_index + 1], value.shape)


def down(value, row_index):
    return jnp.broadcast_to(value[row_index : row_index + 1, :], value.shape)


def tree_sum(terms):
    terms = list(terms)
    while len(terms) > 1:
        terms = [
            terms[at] + terms[at + 1] if at + 1 < len(terms) else terms[at]
            for at in range(0, len(terms), 2)
        ]
    return terms[0]


def dot32(left, right, dims=((1,), (0,))):
    return lax.dot_general(
        left, right, (dims, ((), ())), precision=HIGHEST, preferred_element_type=jnp.float32
    )


def halves(value):
    high = value.astype(jnp.bfloat16)
    return high, (value - high.astype(jnp.float32)).astype(jnp.bfloat16)


def dot_halves(left, right, dims=((1,), (0,))):
    def one(a, b):
        return lax.dot_general(a, b, (dims, ((), ())), preferred_element_type=jnp.float32)

    return one(left[0], right[0]) + (one(left[0], right[1]) + one(left[1], right[0]))


def panel_step(panel, first, lane, sub, ones):
    cols = [across(panel, first + j) * ones for j in range(PANEL)]
    entry = [[None] * PANEL for _ in range(PANEL)]
    for i in range(PANEL):
        for j in range(i, PANEL):
            entry[i][j] = entry[j][i] = down(cols[j], i)
    inside = (lane >= first) & (lane < first + PANEL)
    augmented = jnp.where(inside, jnp.where(lane == first + sub, 1.0, 0.0), panel)
    lower = jnp.where(lane < first + PANEL, augmented, 0.0)
    rows = [down(augmented, i) for i in range(PANEL)]
    for j in range(0, PANEL, 2):
        p, b, s = entry[j][j], entry[j][j + 1], entry[j + 1][j + 1]
        r = 1.0 / (p * s - b * b)
        upper_new, lower_new = {}, {}
        for m in range(j + 2, PANEL):
            upper_new[m] = (s * entry[j][m] - b * entry[j + 1][m]) * r
            lower_new[m] = (p * entry[j + 1][m] - b * entry[j][m]) * r
        upper_row = (s * rows[j] - b * rows[j + 1]) * r
        lower_row = (p * rows[j + 1] - b * rows[j]) * r
        for i in range(PANEL):
            if i in (j, j + 1):
                continue
            f, g = entry[i][j], entry[i][j + 1]
            for m in range(max(j + 2, i if i > j else 0), PANEL):
                value = entry[i][m] - (f * upper_new[m] + g * lower_new[m])
                entry[i][m] = value
                if i > j and m > i:
                    entry[m][i] = value
            rows[i] = rows[i] - (f * upper_row + g * lower_row)
        for m in range(j + 2, PANEL):
            entry[j][m] = upper_new[m]
            entry[j + 1][m] = lower_new[m]
        rows[j], rows[j + 1] = upper_row, lower_row
    solved = rows[0]
    for i in range(1, PANEL):
        solved = jnp.where(sub == i, rows[i], solved)
    return lower, rows, solved, inside


def factor_block(block, lower_ref, scaled_ref, ones):
    count = BLOCK // PANEL
    lane = lax.broadcasted_iota(jnp.int32, (PANEL, BLOCK), 1)
    sub = lax.broadcasted_iota(jnp.int32, (PANEL, BLOCK), 0)
    rows = [block[PANEL * i : PANEL * (i + 1), :] for i in range(count)]
    for q in range(count):
        first = q * PANEL
        lower, pivot_rows, solved, inside = panel_step(rows[q], first, lane, sub, ones)
        lower_ref[first : first + PANEL, :] = lower
        scaled_ref[first : first + PANEL, :] = jnp.where(lane < first + PANEL, solved, 0.0)
        for i in range(q + 1, count):
            change = tree_sum(
                across(rows[i], first + j) * pivot_rows[j] for j in range(PANEL)
            )
            rows[i] = jnp.where(inside, 0.0, rows[i]) - change


SPARE = 16
GROUP = ("space", "obs")


def gauss_jordan(work_ref, out_ref, lower_ref, scaled_ref, ones_ref):
    blocks = work_ref.shape[0] // BLOCK
    ones_ref[...] = jnp.ones_like(ones_ref)
    ones = ones_ref[...]
    current = work_ref[0:BLOCK, 0:BLOCK]
    for p in range(blocks):
        at, after = p * BLOCK, (p + 1) * BLOCK
        last = p == blocks - 1
        slot = p % 2
        factor_block(current, lower_ref.at[slot], scaled_ref.at[slot], ones)
        lower, scaled = lower_ref[slot], scaled_ref[slot]
        lower, scaled = halves(lower), halves(scaled)
        if not last:
            below = dot_halves(
                halves(work_ref[after : after + BLOCK, at:after]), lower, ((1,), (1,))
            )
            beside = dot_halves(scaled, halves(work_ref[at:after, after : after + BLOCK]))
            current = work_ref[after : after + BLOCK, after : after + BLOCK] - dot_halves(
                halves(below), halves(beside)
            )
        inverse = halves(dot_halves(lower, scaled, ((0,), (0,))))
        if not last:
            panel = dot_halves(inverse, halves(work_ref[at:after, after:]))
            panel_parts = halves(panel)
        turned = dot_halves(halves(out_ref[:, at:after]), inverse)
        turned_parts = halves(turned)
        for i in range(blocks):
            if i == p:
                continue
            span = slice(i * BLOCK, (i + 1) * BLOCK)
            column = halves(work_ref[span, at:after])
            if not last:
                work_ref[span, after:] -= dot_halves(column, panel_parts)
            out_ref[:, span] -= dot_halves(turned_parts, column, ((1,), (1,)))
        if not last:
            work_ref[at:after, after:] = panel
        out_ref[:, at:after] = turned


def diagonal_mask(count, nodes, first):
    row_at = lax.broadcasted_iota(jnp.int32, (count, nodes), 0) + first
    return row_at == lax.broadcasted_iota(jnp.int32, (count, nodes), 1)


def to_row(column, mask):
    return jnp.sum(jnp.where(mask, column, 0.0), axis=0, keepdims=True)


def write_packed(ref, start, rows, mask, vectors):
    count, nodes = rows.shape
    high = rows.astype(jnp.bfloat16)
    ref[start : start + count, :] = high
    lines = [to_row(rows - high.astype(jnp.float32), mask)]
    for vector in vectors:
        for _ in range(3):
            part = vector.astype(jnp.bfloat16).astype(jnp.float32)
            lines.append(part)
            vector = vector - part
    place = lax.broadcasted_iota(jnp.int32, (SPARE, nodes), 0)
    spare = jnp.zeros((SPARE, nodes), jnp.float32)
    for at, line in enumerate(lines):
        spare = jnp.where(place == at, jnp.broadcast_to(line, spare.shape), spare)
    ref[start + count : start + count + SPARE, :] = spare.astype(jnp.bfloat16)


def read_spare(ref, start, count):
    return ref[start + count : start + count + SPARE, :].astype(jnp.float32)


def spare_vector(spare, at):
    first = 1 + 3 * at
    return spare[first : first + 1] + (
        spare[first + 1 : first + 2] + spare[first + 2 : first + 3]
    )


def read_rows(ref, start, count, mask):
    rows = ref[start : start + count, :].astype(jnp.float32)
    return rows + jnp.where(mask, read_spare(ref, start, count)[0:1], 0.0)


def partner_product(solved, partner_ref, rest, both=True):
    high, low = halves(solved)

    def one(part):
        return lax.dot_general(
            part, partner_ref[...], (((1,), (1,)), ((), ())), preferred_element_type=jnp.float32
        )

    found = one(high) + solved * rest
    return found + one(low) if both else found


def pack_kernel(cells_ref, rows_ref, coef_ref, prior_ref, out_ref):
    count, nodes = rows_ref.shape
    mask = diagonal_mask(count, nodes, cells_ref[0] * count)
    lane = lax.broadcasted_iota(jnp.int32, (1, nodes), 1)
    coef = jnp.where(lane == 0, jnp.broadcast_to(coef_ref[...], (1, nodes)), 0.0)
    prior = dot32(jnp.broadcast_to(prior_ref[...], (8, count)), mask.astype(jnp.float32))[0:1]
    write_packed(out_ref, 0, rows_ref[...], mask, (coef, prior))


def first_kernel(n_cells, cells_ref, coef_ref, prec_ref, gram_ref, *refs):
    own_refs, next_refs = refs[:n_cells], refs[n_cells : 2 * n_cells]
    sent_refs, fill_ref, diag_ref, rhs_ref = refs[2 * n_cells : 2 * n_cells + 4], *refs[
        2 * n_cells + 4 : 2 * n_cells + 7
    ]
    work_ref, out_ref, own_all, next_all, lower_ref, scaled_ref, ones_ref = refs[
        2 * n_cells + 7 :
    ]
    count, nodes = prec_ref.shape
    own_coef = coef_ref[...]
    next_spare = read_spare(next_refs[0], 0, count)
    next_coef = spare_vector(next_spare, 0)[:, 0:1]
    square = next_coef * next_coef
    own_rest = jnp.zeros((1, nodes), jnp.float32)
    next_rest = jnp.zeros((1, nodes), jnp.float32)
    rhs = gram_ref[nodes : nodes + 1, :] + gram_ref[nodes + 1 : nodes + 2, :]
    for k in range(n_cells):
        first = pl.multiple_of(cells_ref[k] * count, SPARE)
        span = pl.ds(first, count)
        mask = diagonal_mask(count, nodes, first)
        own_spare = read_spare(own_refs[k], 0, count)
        own_rest = own_rest + own_spare[0:1]
        next_rest = next_rest + read_spare(next_refs[k], 0, count)[0:1]
        prior = spare_vector(own_spare, 1)
        rhs = rhs + prior
        own_high, next_high = own_refs[k][0:count, :], next_refs[k][0:count, :]
        own_all[span, :] = own_high
        next_all[span, :] = next_high
        own_rows = read_rows(own_refs[k], 0, count, mask)
        next_rows = read_rows(next_refs[k], 0, count, mask)
        if k == 0:
            own_rows = prec_ref[...]
        rows = own_rows + square * next_rows + gram_ref[span, :]
        work_ref[span, :] = rows
        if k == 0:
            my_mask = mask
            diag_ref[...] = rows
            out_ref[0:count, :] = -own_coef * own_rows
            out_ref[count : 2 * count, :] = -next_coef * next_rows
    my_columns = jnp.sum(jnp.where(my_mask, 1.0, 0.0), axis=0, keepdims=True)
    rhs_ref[...] = jnp.broadcast_to(jnp.where(my_columns > 0.5, rhs, 0.0), rhs_ref.shape)
    gauss_jordan(work_ref, out_ref, lower_ref, scaled_ref, ones_ref)
    solved = out_ref[...]
    up = jnp.sum(solved * rhs, axis=1, keepdims=True)
    left = -own_coef * partner_product(solved, own_all, own_rest)
    right = -next_coef * partner_product(solved, next_all, next_rest)
    up_left, up_right = to_row(up[:count], my_mask), to_row(up[count:], my_mask)
    write_packed(sent_refs[0], 0, right[count:], my_mask, (up_right,))
    write_packed(sent_refs[1], 0, left[:count], my_mask, (up_left,))
    write_packed(sent_refs[2], 0, -right[:count], my_mask, ())
    write_packed(sent_refs[3], 0, -left[count:], my_mask, ())
    fill_ref[...] = -right[:count]


def merge_kernel(cells_ref, diag_ref, rhs_ref, left_ref, right_ref, pack_ref, out_ref, out_rhs):
    count, nodes = diag_ref.shape
    mask = diagonal_mask(count, nodes, cells_ref[0] * count)
    rows = (
        diag_ref[...] - read_rows(left_ref, 0, count, mask) - read_rows(right_ref, 0, count, mask)
    )
    rhs = (
        rhs_ref[0:1]
        - spare_vector(read_spare(left_ref, 0, count), 0)
        - spare_vector(read_spare(right_ref, 0, count), 0)
    )
    out_ref[...] = rows
    out_rhs[...] = jnp.broadcast_to(rhs, out_rhs.shape)
    write_packed(pack_ref, 0, rows, mask, (rhs,))


def second_kernel(n_cells, cells_ref, partner_ref, *refs):
    diag_refs = refs[:n_cells]
    out_ref, rhs_ref, work_ref, lower_ref, scaled_ref, ones_ref = refs[n_cells:]
    count = diag_refs[0].shape[0] - SPARE
    nodes = diag_refs[0].shape[1]
    size = count + SPARE
    rhs = jnp.zeros((1, nodes), jnp.float32)
    for k in range(n_cells):
        first = pl.multiple_of(cells_ref[k] * count, SPARE)
        mask = diagonal_mask(count, nodes, first)
        work_ref[pl.ds(first, count), :] = read_rows(diag_refs[k], 0, count, mask)
        rhs = rhs + spare_vector(read_spare(diag_refs[k], 0, count), 0)
        if k == 0:
            out_ref[0:count, :] = read_rows(partner_ref, 0, count, mask)
            out_ref[count : 2 * count, :] = read_rows(partner_ref, size, count, mask)
    rhs_ref[...] = jnp.broadcast_to(rhs, rhs_ref.shape)
    gauss_jordan(work_ref, out_ref, lower_ref, scaled_ref, ones_ref)


def last_kernel(n_cells, together, cells_ref, solved_ref, rhs_ref, *refs):
    pieces = refs[:n_cells]
    loss_ref, fill_ref, left_all, right_all = refs[n_cells:]
    nodes = solved_ref.shape[1]
    count = solved_ref.shape[0] // 2
    size = count + SPARE
    rests = [jnp.zeros((1, nodes), jnp.float32), jnp.zeros((1, nodes), jnp.float32)]
    for k in range(n_cells):
        span = pl.ds(pl.multiple_of(cells_ref[k] * count, SPARE), count)
        for side, target in enumerate((left_all, right_all)):
            start = side * size
            target[span, :] = pieces[k][start : start + count, :]
            rests[side] = rests[side] + read_spare(pieces[k], start, count)[0:1]
    mask = diagonal_mask(count, nodes, cells_ref[0] * count)
    solved = solved_ref[...]
    up = jnp.sum(solved * rhs_ref[0:1], axis=1, keepdims=True)
    up_left, up_right = to_row(up[:count], mask), to_row(up[count:], mask)
    left = partner_product(solved[:count], left_all, rests[0], both=False)
    right = partner_product(solved, right_all, rests[1], both=False)
    if together:
        write_packed(loss_ref, 0, left + right[count:], mask, (up_left + up_right,))
    else:
        write_packed(loss_ref, 0, left, mask, (up_left,))
        write_packed(loss_ref, size, right[count:], mask, (up_right,))
    fill_ref[...] = -right[:count]


def on_chip(kernel, name, out_shapes, scratch, operands, flops):
    vmem = pl.BlockSpec(memory_space=pltpu.VMEM)
    cells = pl.BlockSpec(memory_space=pltpu.SMEM)
    return pl.pallas_call(
        kernel,
        out_shape=[jax.ShapeDtypeStruct(shape, dtype) for shape, dtype in out_shapes],
        in_specs=[cells] + [vmem] * (len(operands) - 1),
        out_specs=[vmem] * len(out_shapes),
        scratch_shapes=[pltpu.VMEM(shape, dtype) for shape, dtype in scratch],
        cost_estimate=pl.CostEstimate(flops=flops, bytes_accessed=1 << 20, transcendentals=0),
        name=name,
    )(*operands)


def solve_scratch():
    return [
        ((2, BLOCK, BLOCK), jnp.float32),
        ((2, BLOCK, BLOCK), jnp.float32),
        ((PANEL, BLOCK), jnp.float32),
    ]


def shift(value, axis, steps, sources=None):
    count = lax.axis_size(axis)
    pairs = [
        (source, (source + steps) % count)
        for source in range(count)
        if sources is None or sources(source)
    ]
    return lax.ppermute(value, axis, pairs)


def cell_shifts():
    n_space, n_obs = lax.axis_size("space"), lax.axis_size("obs")
    return [(d, e) for e in range(n_obs) for d in range(n_space)]


def cell_table():
    n_space, n_obs = lax.axis_size("space"), lax.axis_size("obs")
    my_space, my_obs = lax.axis_index("space"), lax.axis_index("obs")
    cells = [
        lax.rem(my_space - d + n_space, n_space) * n_obs + lax.rem(my_obs - e + n_obs, n_obs)
        for d, e in cell_shifts()
    ]
    return jnp.stack(cells).astype(jnp.int32)


def spread(value):
    n_space, n_obs = lax.axis_size("space"), lax.axis_size("obs")
    along = [value] + [shift(value, "space", d) for d in range(1, n_space)]
    pieces = list(along)
    for e in range(1, n_obs):
        pieces += [shift(part, "obs", e) for part in along]
    return pieces


def spread_at_once(value):
    n_space, n_obs = lax.axis_size("space"), lax.axis_size("obs")
    pieces = []
    for d, e in cell_shifts()[1:]:
        pairs = [
            (s * n_obs + o, ((s + d) % n_space) * n_obs + (o + e) % n_obs)
            for s in range(n_space)
            for o in range(n_obs)
        ]
        pieces.append(lax.ppermute(value, GROUP, pairs))
    return pieces


def rounded(value):
    return lax.reduce_precision(value, 8, 7)


def unpack_rows(packed, mask):
    count = packed.shape[0] - SPARE
    rows = packed[:count].astype(jnp.float32)
    return rows + jnp.where(mask, packed[count].astype(jnp.float32)[None, :], 0.0)


def unpack_vector(packed):
    first = packed.shape[0] - SPARE + 1
    parts = packed[first : first + 3].astype(jnp.float32)
    return parts[0] + (parts[1] + parts[2])


def routed_rows(obs_panel, node_index, weight, residual, route_time, n_times):
    rows_dev, nodes = obs_panel.shape
    capacity = 2 * rows_dev // n_times
    root = jnp.sqrt(weight.astype(jnp.float32))
    node_hits = node_index[:, None] == lax.iota(jnp.int32, nodes)[None, :]
    design = rounded(obs_panel.astype(jnp.float32) + node_hits.astype(jnp.float32))
    scaled = (root[:, None] * design).astype(jnp.bfloat16)
    target = root * residual.astype(jnp.float32)
    target_high = rounded(target)
    same = route_time[:, None] == route_time[None, :]
    earlier = lax.iota(jnp.int32, rows_dev)[:, None] > lax.iota(jnp.int32, rows_dev)[None, :]
    rank = jnp.sum((same & earlier).astype(jnp.int32), axis=1)
    ahead = lax.rem(route_time - lax.axis_index("tm") + n_times, n_times)
    column = lax.iota(jnp.int32, SPARE)[None, :]
    extra = jnp.where(
        column == 0,
        target_high[:, None],
        jnp.where(column == 1, (target - target_high)[:, None], 0.0),
    ).astype(jnp.bfloat16)
    rows = jnp.concatenate([scaled, extra], axis=1)
    slots = lax.iota(jnp.int32, capacity)[None, :]
    parts = []
    for step in range(n_times):
        slot_of = (ahead[:, None] == step) & (rank[:, None] == slots)
        part = lax.dot_general(
            rows,
            slot_of.astype(jnp.bfloat16),
            (((0,), (0,)), ((), ())),
            preferred_element_type=jnp.float32,
        ).astype(jnp.bfloat16)
        parts.append(shift(part, "tm", step) if step else part)
    return parts


def moments(slots, nodes):
    return lax.dot_general(
        slots, slots[:nodes], (((1,), (1,)), ((), ())), preferred_element_type=jnp.float32
    )


def local(obs_panel, node_index, weight, residual, route_time, spatial_prec, ar_coef, prior_rhs):
    n_times = lax.axis_size("tm")
    n_space, n_obs = lax.axis_size("space"), lax.axis_size("obs")
    n_cells = n_space * n_obs
    time_index = lax.axis_index("tm")
    nodes = obs_panel.shape[1]
    count = spatial_prec.shape[1]
    size = count + SPARE
    assert nodes % BLOCK == 0 and count % SPARE == 0
    cells = cell_table()
    first_row = cells[0] * count
    own_prec, coef = spatial_prec[0], ar_coef.reshape(1, 1)
    (own_pack,) = on_chip(
        pack_kernel,
        "pack_prior",
        [((size, nodes), jnp.bfloat16)],
        [],
        (cells, own_prec, coef, prior_rhs),
        0,
    )
    own_pack, route_time = lax.optimization_barrier((own_pack, route_time))
    from_next = shift(own_pack, "tm", -1)
    own_pieces = spread(own_pack)
    parts = routed_rows(obs_panel, node_index, weight, residual, route_time, n_times)
    next_pieces = spread(from_next)
    own_slots = [shift(parts[0], "space", d) for d in range(1, n_space)]
    before = (own_pieces[:n_space], next_pieces[:n_space], own_slots)
    for step in range(1, n_times):
        parts[step], before = lax.optimization_barrier((parts[step], before))
    own_pieces[:n_space], next_pieces[:n_space], own_slots = before

    arrived = jnp.concatenate(parts, axis=1)
    near = [arrived] + [shift(arrived, "obs", e) for e in range(1, n_obs)]
    gram = sum(moments(part, nodes) for part in near)
    for d in range(1, n_space):
        slots = [own_slots[d - 1]] + [shift(part, "space", d) for part in parts[1:]]
        slots, gram = lax.optimization_barrier((slots, gram))
        far = jnp.concatenate(slots, axis=1)
        gram = gram + moments(far, nodes)
        for e in range(1, n_obs):
            gram = gram + moments(shift(far, "obs", e), nodes)

    loss_right, loss_left, pack_fill, pack_turn, fill_one, diag_one, rhs_one = on_chip(
        functools.partial(first_kernel, n_cells),
        "level_one",
        [((size, nodes), jnp.bfloat16)] * 4
        + [
            ((count, nodes), jnp.float32),
            ((count, nodes), jnp.float32),
            ((8, nodes), jnp.float32),
        ],
        [
            ((nodes, nodes), jnp.float32),
            ((2 * count, nodes), jnp.float32),
            ((nodes, nodes), jnp.bfloat16),
            ((nodes, nodes), jnp.bfloat16),
        ]
        + solve_scratch(),
        (cells, coef, own_prec, gram, *own_pieces, *next_pieces),
        70 * nodes**3,
    )
    def is_second(time):
        return time % 4 == 2

    def after_one(time):
        return time % 4 == 1

    def before_none(time):
        return time % 4 == 3

    came_left = shift(loss_right, "tm", 1, after_one)
    came_right = shift(loss_left, "tm", -1, before_none)
    pack_fill, pack_turn, came_left, came_right = lax.optimization_barrier(
        (pack_fill, pack_turn, came_left, came_right)
    )
    fill_left = shift(pack_fill, "tm", 1, after_one)
    fill_right = shift(pack_turn, "tm", -1, before_none)

    pack_two, diag_two, rhs_two = on_chip(
        merge_kernel,
        "merge_losses",
        [
            ((size, nodes), jnp.bfloat16),
            ((count, nodes), jnp.float32),
            ((8, nodes), jnp.float32),
        ],
        [],
        (cells, diag_one, rhs_one, came_left, came_right),
        0,
    )
    pieces_two = spread(pack_two)
    fill_left, fill_right, pieces_two[0], loss_right, loss_left = lax.optimization_barrier(
        (fill_left, fill_right, pieces_two[0], loss_right, loss_left)
    )
    partner = jnp.concatenate([fill_left, fill_right], axis=0)
    partners = spread_at_once(partner)
    late_left = shift(loss_right, "tm", 1, before_none)
    late_right = shift(loss_left, "tm", -1, after_one)
    solved, rhs_full = on_chip(
        functools.partial(second_kernel, n_cells),
        "level_two",
        [((2 * count, nodes), jnp.float32), ((8, nodes), jnp.float32)],
        [((nodes, nodes), jnp.float32)] + solve_scratch(),
        (cells, partner, *pieces_two),
        60 * nodes**3,
    )
    together = 4 % n_times == 0
    loss_two, fill_two = on_chip(
        functools.partial(last_kernel, n_cells, together),
        "products_two",
        [
            ((size if together else 2 * size, nodes), jnp.bfloat16),
            ((count, nodes), jnp.float32),
        ],
        [((nodes, nodes), jnp.bfloat16), ((nodes, nodes), jnp.bfloat16)],
        (cells, solved, rhs_full, partner, *partners),
        4 * nodes**3,
    )

    if together:
        came = [shift(loss_two, "tm", 2, is_second)]
    else:
        came = [
            shift(loss_two[:size], "tm", -2, is_second),
            shift(loss_two[size:], "tm", 2, is_second),
        ]
    mask = diagonal_mask(count, nodes, first_row)
    diag_out = diag_two - unpack_rows(late_left, mask) - unpack_rows(late_right, mask)
    rhs_out = rhs_two[0] - unpack_vector(late_left) - unpack_vector(late_right)
    for part in came:
        diag_out = diag_out - unpack_rows(part, mask)
        rhs_out = rhs_out - unpack_vector(part)
    rhs_out = lax.dynamic_slice_in_dim(rhs_out, first_row, count, 0)
    fill_out = jnp.where(
        time_index % 2 == 1,
        fill_one,
        jnp.where(is_second(time_index), fill_two, jnp.zeros_like(fill_two)),
    )
    return (diag_out[None], fill_out[None], rhs_out[None])


def solution(mesh):
    return jax.shard_map(
        local,
        mesh=mesh,
        in_specs=(
            P(("grp", "tm", "space", "obs"), None),
            P(("grp", "tm", "space", "obs")),
            P(("grp", "tm", "space", "obs")),
            P(("grp", "tm", "space", "obs")),
            P(("grp", "tm", "space", "obs")),
            P(("grp", "tm"), ("space", "obs"), None),
            P(("grp", "tm")),
            P(("grp", "tm"), ("space", "obs")),
        ),
        out_specs=(
            P(("grp", "tm"), ("space", "obs"), None),
            P(("grp", "tm"), ("space", "obs"), None),
            P(("grp", "tm"), ("space", "obs")),
        ),
        check_vma=False,
    )
```

```python
import functools

import jax
import jax.numpy as jnp
from jax import lax
from jax.experimental import pallas as pl
from jax.experimental.pallas import tpu as pltpu
from jax.sharding import PartitionSpec as P


BLOCK = 128
PANEL = 8
HIGHEST = lax.Precision.HIGHEST


def across(value, lane_index):
    return jnp.broadcast_to(value[:, lane_index : lane_index + 1], value.shape)


def down(value, row_index):
    return jnp.broadcast_to(value[row_index : row_index + 1, :], value.shape)


def tree_sum(terms):
    terms = list(terms)
    while len(terms) > 1:
        terms = [
            terms[at] + terms[at + 1] if at + 1 < len(terms) else terms[at]
            for at in range(0, len(terms), 2)
        ]
    return terms[0]


def dot32(left, right, dims=((1,), (0,))):
    return lax.dot_general(
        left, right, (dims, ((), ())), precision=HIGHEST, preferred_element_type=jnp.float32
    )


def halves(value):
    high = value.astype(jnp.bfloat16)
    return high, (value - high.astype(jnp.float32)).astype(jnp.bfloat16)


def dot_halves(left, right, dims=((1,), (0,))):
    def one(a, b):
        return lax.dot_general(a, b, (dims, ((), ())), preferred_element_type=jnp.float32)

    return one(left[0], right[0]) + (one(left[0], right[1]) + one(left[1], right[0]))


def panel_step(panel, first, lane, sub, ones):
    cols = [across(panel, first + j) * ones for j in range(PANEL)]
    entry = [[None] * PANEL for _ in range(PANEL)]
    for i in range(PANEL):
        for j in range(i, PANEL):
            entry[i][j] = entry[j][i] = down(cols[j], i)
    inside = (lane >= first) & (lane < first + PANEL)
    augmented = jnp.where(inside, jnp.where(lane == first + sub, 1.0, 0.0), panel)
    lower = jnp.where(lane < first + PANEL, augmented, 0.0)
    rows = [down(augmented, i) for i in range(PANEL)]
    for j in range(0, PANEL, 2):
        p, b, s = entry[j][j], entry[j][j + 1], entry[j + 1][j + 1]
        r = 1.0 / (p * s - b * b)
        upper_new, lower_new = {}, {}
        for m in range(j + 2, PANEL):
            upper_new[m] = (s * entry[j][m] - b * entry[j + 1][m]) * r
            lower_new[m] = (p * entry[j + 1][m] - b * entry[j][m]) * r
        upper_row = (s * rows[j] - b * rows[j + 1]) * r
        lower_row = (p * rows[j + 1] - b * rows[j]) * r
        for i in range(PANEL):
            if i in (j, j + 1):
                continue
            f, g = entry[i][j], entry[i][j + 1]
            for m in range(max(j + 2, i if i > j else 0), PANEL):
                value = entry[i][m] - (f * upper_new[m] + g * lower_new[m])
                entry[i][m] = value
                if i > j and m > i:
                    entry[m][i] = value
            rows[i] = rows[i] - (f * upper_row + g * lower_row)
        for m in range(j + 2, PANEL):
            entry[j][m] = upper_new[m]
            entry[j + 1][m] = lower_new[m]
        rows[j], rows[j + 1] = upper_row, lower_row
    solved = rows[0]
    for i in range(1, PANEL):
        solved = jnp.where(sub == i, rows[i], solved)
    return lower, rows, solved, inside


def factor_block(block, lower_ref, scaled_ref, ones):
    count = BLOCK // PANEL
    lane = lax.broadcasted_iota(jnp.int32, (PANEL, BLOCK), 1)
    sub = lax.broadcasted_iota(jnp.int32, (PANEL, BLOCK), 0)
    rows = [block[PANEL * i : PANEL * (i + 1), :] for i in range(count)]
    for q in range(count):
        first = q * PANEL
        lower, pivot_rows, solved, inside = panel_step(rows[q], first, lane, sub, ones)
        lower_ref[first : first + PANEL, :] = lower
        scaled_ref[first : first + PANEL, :] = jnp.where(lane < first + PANEL, solved, 0.0)
        for i in range(q + 1, count):
            change = tree_sum(
                across(rows[i], first + j) * pivot_rows[j] for j in range(PANEL)
            )
            rows[i] = jnp.where(inside, 0.0, rows[i]) - change


SPARE = 16
GROUP = ("space", "obs")


def gauss_jordan(work_ref, out_ref, lower_ref, scaled_ref, ones_ref):
    blocks = work_ref.shape[0] // BLOCK
    ones_ref[...] = jnp.ones_like(ones_ref)
    ones = ones_ref[...]
    current = work_ref[0:BLOCK, 0:BLOCK]
    for p in range(blocks):
        at, after = p * BLOCK, (p + 1) * BLOCK
        last = p == blocks - 1
        slot = p % 2
        factor_block(current, lower_ref.at[slot], scaled_ref.at[slot], ones)
        lower, scaled = lower_ref[slot], scaled_ref[slot]
        lower, scaled = halves(lower), halves(scaled)
        if not last:
            below = dot_halves(
                halves(work_ref[after : after + BLOCK, at:after]), lower, ((1,), (1,))
            )
            beside = dot_halves(scaled, halves(work_ref[at:after, after : after + BLOCK]))
            current = work_ref[after : after + BLOCK, after : after + BLOCK] - dot_halves(
                halves(below), halves(beside)
            )
        inverse = halves(dot_halves(lower, scaled, ((0,), (0,))))
        if not last:
            panel = dot_halves(inverse, halves(work_ref[at:after, after:]))
            panel_parts = halves(panel)
        turned = dot_halves(halves(out_ref[:, at:after]), inverse)
        turned_parts = halves(turned)
        for i in range(blocks):
            if i == p:
                continue
            span = slice(i * BLOCK, (i + 1) * BLOCK)
            column = halves(work_ref[span, at:after])
            if not last:
                work_ref[span, after:] -= dot_halves(column, panel_parts)
            out_ref[:, span] -= dot_halves(turned_parts, column, ((1,), (1,)))
        if not last:
            work_ref[at:after, after:] = panel
        out_ref[:, at:after] = turned


def diagonal_mask(count, nodes, first):
    row_at = lax.broadcasted_iota(jnp.int32, (count, nodes), 0) + first
    return row_at == lax.broadcasted_iota(jnp.int32, (count, nodes), 1)


def to_row(column, mask):
    return jnp.sum(jnp.where(mask, column, 0.0), axis=0, keepdims=True)


def write_packed(ref, start, rows, mask, vectors):
    count, nodes = rows.shape
    high = rows.astype(jnp.bfloat16)
    ref[start : start + count, :] = high
    lines = [to_row(rows - high.astype(jnp.float32), mask)]
    for vector in vectors:
        for _ in range(3):
            part = vector.astype(jnp.bfloat16).astype(jnp.float32)
            lines.append(part)
            vector = vector - part
    place = lax.broadcasted_iota(jnp.int32, (SPARE, nodes), 0)
    spare = jnp.zeros((SPARE, nodes), jnp.float32)
    for at, line in enumerate(lines):
        spare = jnp.where(place == at, jnp.broadcast_to(line, spare.shape), spare)
    ref[start + count : start + count + SPARE, :] = spare.astype(jnp.bfloat16)


def read_spare(ref, start, count):
    return ref[start + count : start + count + SPARE, :].astype(jnp.float32)


def spare_vector(spare, at):
    first = 1 + 3 * at
    return spare[first : first + 1] + (
        spare[first + 1 : first + 2] + spare[first + 2 : first + 3]
    )


def read_rows(ref, start, count, mask):
    rows = ref[start : start + count, :].astype(jnp.float32)
    return rows + jnp.where(mask, read_spare(ref, start, count)[0:1], 0.0)


def partner_product(solved, partner_ref, rest, both=True):
    high, low = halves(solved)

    def one(part):
        return lax.dot_general(
            part, partner_ref[...], (((1,), (1,)), ((), ())), preferred_element_type=jnp.float32
        )

    found = one(high) + solved * rest
    return found + one(low) if both else found


def pack_kernel(cells_ref, rows_ref, coef_ref, prior_ref, out_ref):
    count, nodes = rows_ref.shape
    mask = diagonal_mask(count, nodes, cells_ref[0] * count)
    lane = lax.broadcasted_iota(jnp.int32, (1, nodes), 1)
    coef = jnp.where(lane == 0, jnp.broadcast_to(coef_ref[...], (1, nodes)), 0.0)
    prior = dot32(jnp.broadcast_to(prior_ref[...], (8, count)), mask.astype(jnp.float32))[0:1]
    write_packed(out_ref, 0, rows_ref[...], mask, (coef, prior))


def first_kernel(n_cells, cells_ref, coef_ref, prec_ref, gram_ref, *refs):
    own_refs, next_refs = refs[:n_cells], refs[n_cells : 2 * n_cells]
    sent_refs, fill_ref, diag_ref, rhs_ref = refs[2 * n_cells : 2 * n_cells + 4], *refs[
        2 * n_cells + 4 : 2 * n_cells + 7
    ]
    work_ref, out_ref, own_all, next_all, lower_ref, scaled_ref, ones_ref = refs[
        2 * n_cells + 7 :
    ]
    count, nodes = prec_ref.shape
    own_coef = coef_ref[...]
    next_spare = read_spare(next_refs[0], 0, count)
    next_coef = spare_vector(next_spare, 0)[:, 0:1]
    square = next_coef * next_coef
    own_rest = jnp.zeros((1, nodes), jnp.float32)
    next_rest = jnp.zeros((1, nodes), jnp.float32)
    rhs = gram_ref[nodes : nodes + 1, :] + gram_ref[nodes + 1 : nodes + 2, :]
    for k in range(n_cells):
        first = pl.multiple_of(cells_ref[k] * count, SPARE)
        span = pl.ds(first, count)
        mask = diagonal_mask(count, nodes, first)
        own_spare = read_spare(own_refs[k], 0, count)
        own_rest = own_rest + own_spare[0:1]
        next_rest = next_rest + read_spare(next_refs[k], 0, count)[0:1]
        prior = spare_vector(own_spare, 1)
        rhs = rhs + prior
        own_high, next_high = own_refs[k][0:count, :], next_refs[k][0:count, :]
        own_all[span, :] = own_high
        next_all[span, :] = next_high
        own_rows = read_rows(own_refs[k], 0, count, mask)
        next_rows = read_rows(next_refs[k], 0, count, mask)
        if k == 0:
            own_rows = prec_ref[...]
        rows = own_rows + square * next_rows + gram_ref[span, :]
        work_ref[span, :] = rows
        if k == 0:
            my_mask = mask
            diag_ref[...] = rows
            out_ref[0:count, :] = -own_coef * own_rows
            out_ref[count : 2 * count, :] = -next_coef * next_rows
    my_columns = jnp.sum(jnp.where(my_mask, 1.0, 0.0), axis=0, keepdims=True)
    rhs_ref[...] = jnp.broadcast_to(jnp.where(my_columns > 0.5, rhs, 0.0), rhs_ref.shape)
    gauss_jordan(work_ref, out_ref, lower_ref, scaled_ref, ones_ref)
    solved = out_ref[...]
    up = jnp.sum(solved * rhs, axis=1, keepdims=True)
    left = -own_coef * partner_product(solved, own_all, own_rest)
    right = -next_coef * partner_product(solved, next_all, next_rest)
    up_left, up_right = to_row(up[:count], my_mask), to_row(up[count:], my_mask)
    write_packed(sent_refs[0], 0, right[count:], my_mask, (up_right,))
    write_packed(sent_refs[1], 0, left[:count], my_mask, (up_left,))
    write_packed(sent_refs[2], 0, -right[:count], my_mask, ())
    write_packed(sent_refs[3], 0, -left[count:], my_mask, ())
    fill_ref[...] = -right[:count]


def merge_kernel(cells_ref, diag_ref, rhs_ref, left_ref, right_ref, pack_ref, out_ref, out_rhs):
    count, nodes = diag_ref.shape
    mask = diagonal_mask(count, nodes, cells_ref[0] * count)
    rows = (
        diag_ref[...] - read_rows(left_ref, 0, count, mask) - read_rows(right_ref, 0, count, mask)
    )
    rhs = (
        rhs_ref[0:1]
        - spare_vector(read_spare(left_ref, 0, count), 0)
        - spare_vector(read_spare(right_ref, 0, count), 0)
    )
    out_ref[...] = rows
    out_rhs[...] = jnp.broadcast_to(rhs, out_rhs.shape)
    write_packed(pack_ref, 0, rows, mask, (rhs,))


def second_kernel(n_cells, cells_ref, partner_ref, *refs):
    diag_refs = refs[:n_cells]
    out_ref, rhs_ref, work_ref, lower_ref, scaled_ref, ones_ref = refs[n_cells:]
    count = diag_refs[0].shape[0] - SPARE
    nodes = diag_refs[0].shape[1]
    size = count + SPARE
    rhs = jnp.zeros((1, nodes), jnp.float32)
    for k in range(n_cells):
        first = pl.multiple_of(cells_ref[k] * count, SPARE)
        mask = diagonal_mask(count, nodes, first)
        work_ref[pl.ds(first, count), :] = read_rows(diag_refs[k], 0, count, mask)
        rhs = rhs + spare_vector(read_spare(diag_refs[k], 0, count), 0)
        if k == 0:
            out_ref[0:count, :] = read_rows(partner_ref, 0, count, mask)
            out_ref[count : 2 * count, :] = read_rows(partner_ref, size, count, mask)
    rhs_ref[...] = jnp.broadcast_to(rhs, rhs_ref.shape)
    gauss_jordan(work_ref, out_ref, lower_ref, scaled_ref, ones_ref)


def last_kernel(n_cells, together, cells_ref, solved_ref, rhs_ref, *refs):
    pieces = refs[:n_cells]
    loss_ref, fill_ref, left_all, right_all = refs[n_cells:]
    nodes = solved_ref.shape[1]
    count = solved_ref.shape[0] // 2
    size = count + SPARE
    rests = [jnp.zeros((1, nodes), jnp.float32), jnp.zeros((1, nodes), jnp.float32)]
    for k in range(n_cells):
        span = pl.ds(pl.multiple_of(cells_ref[k] * count, SPARE), count)
        for side, target in enumerate((left_all, right_all)):
            start = side * size
            target[span, :] = pieces[k][start : start + count, :]
            rests[side] = rests[side] + read_spare(pieces[k], start, count)[0:1]
    mask = diagonal_mask(count, nodes, cells_ref[0] * count)
    solved = solved_ref[...]
    up = jnp.sum(solved * rhs_ref[0:1], axis=1, keepdims=True)
    up_left, up_right = to_row(up[:count], mask), to_row(up[count:], mask)
    left = partner_product(solved[:count], left_all, rests[0], both=False)
    right = partner_product(solved, right_all, rests[1], both=False)
    if together:
        write_packed(loss_ref, 0, left + right[count:], mask, (up_left + up_right,))
    else:
        write_packed(loss_ref, 0, left, mask, (up_left,))
        write_packed(loss_ref, size, right[count:], mask, (up_right,))
    fill_ref[...] = -right[:count]


def on_chip(kernel, name, out_shapes, scratch, operands, flops):
    vmem = pl.BlockSpec(memory_space=pltpu.VMEM)
    cells = pl.BlockSpec(memory_space=pltpu.SMEM)
    return pl.pallas_call(
        kernel,
        out_shape=[jax.ShapeDtypeStruct(shape, dtype) for shape, dtype in out_shapes],
        in_specs=[cells] + [vmem] * (len(operands) - 1),
        out_specs=[vmem] * len(out_shapes),
        scratch_shapes=[pltpu.VMEM(shape, dtype) for shape, dtype in scratch],
        cost_estimate=pl.CostEstimate(flops=flops, bytes_accessed=1 << 20, transcendentals=0),
        name=name,
    )(*operands)


def solve_scratch():
    return [
        ((2, BLOCK, BLOCK), jnp.float32),
        ((2, BLOCK, BLOCK), jnp.float32),
        ((PANEL, BLOCK), jnp.float32),
    ]


def shift(value, axis, steps, sources=None):
    count = lax.axis_size(axis)
    pairs = [
        (source, (source + steps) % count)
        for source in range(count)
        if sources is None or sources(source)
    ]
    return lax.ppermute(value, axis, pairs)


def cell_shifts():
    n_space, n_obs = lax.axis_size("space"), lax.axis_size("obs")
    return [(d, e) for e in range(n_obs) for d in range(n_space)]


def cell_table():
    n_space, n_obs = lax.axis_size("space"), lax.axis_size("obs")
    my_space, my_obs = lax.axis_index("space"), lax.axis_index("obs")
    cells = [
        lax.rem(my_space - d + n_space, n_space) * n_obs + lax.rem(my_obs - e + n_obs, n_obs)
        for d, e in cell_shifts()
    ]
    return jnp.stack(cells).astype(jnp.int32)


def spread(value):
    n_space, n_obs = lax.axis_size("space"), lax.axis_size("obs")
    along = [value] + [shift(value, "space", d) for d in range(1, n_space)]
    pieces = list(along)
    for e in range(1, n_obs):
        pieces += [shift(part, "obs", e) for part in along]
    return pieces


def spread_at_once(value):
    n_space, n_obs = lax.axis_size("space"), lax.axis_size("obs")
    pieces = []
    for d, e in cell_shifts()[1:]:
        pairs = [
            (s * n_obs + o, ((s + d) % n_space) * n_obs + (o + e) % n_obs)
            for s in range(n_space)
            for o in range(n_obs)
        ]
        pieces.append(lax.ppermute(value, GROUP, pairs))
    return pieces


def rounded(value):
    return lax.reduce_precision(value, 8, 7)


def unpack_rows(packed, mask):
    count = packed.shape[0] - SPARE
    rows = packed[:count].astype(jnp.float32)
    return rows + jnp.where(mask, packed[count].astype(jnp.float32)[None, :], 0.0)


def unpack_vector(packed):
    first = packed.shape[0] - SPARE + 1
    parts = packed[first : first + 3].astype(jnp.float32)
    return parts[0] + (parts[1] + parts[2])


def routed_rows(obs_panel, node_index, weight, residual, route_time, n_times):
    rows_dev, nodes = obs_panel.shape
    capacity = 2 * rows_dev // n_times
    root = jnp.sqrt(weight.astype(jnp.float32))
    node_hits = node_index[:, None] == lax.iota(jnp.int32, nodes)[None, :]
    design = rounded(obs_panel.astype(jnp.float32) + node_hits.astype(jnp.float32))
    scaled = (root[:, None] * design).astype(jnp.bfloat16)
    target = root * residual.astype(jnp.float32)
    target_high = rounded(target)
    same = route_time[:, None] == route_time[None, :]
    earlier = lax.iota(jnp.int32, rows_dev)[:, None] > lax.iota(jnp.int32, rows_dev)[None, :]
    rank = jnp.sum((same & earlier).astype(jnp.int32), axis=1)
    ahead = lax.rem(route_time - lax.axis_index("tm") + n_times, n_times)
    column = lax.iota(jnp.int32, SPARE)[None, :]
    extra = jnp.where(
        column == 0,
        target_high[:, None],
        jnp.where(column == 1, (target - target_high)[:, None], 0.0),
    ).astype(jnp.bfloat16)
    rows = jnp.concatenate([scaled, extra], axis=1)
    slots = lax.iota(jnp.int32, capacity)[None, :]
    parts = []
    for step in range(n_times):
        slot_of = (ahead[:, None] == step) & (rank[:, None] == slots)
        part = lax.dot_general(
            rows,
            slot_of.astype(jnp.bfloat16),
            (((0,), (0,)), ((), ())),
            preferred_element_type=jnp.float32,
        ).astype(jnp.bfloat16)
        parts.append(shift(part, "tm", step) if step else part)
    return parts


def moments(slots, nodes):
    return lax.dot_general(
        slots, slots[:nodes], (((1,), (1,)), ((), ())), preferred_element_type=jnp.float32
    )


def local(obs_panel, node_index, weight, residual, route_time, spatial_prec, ar_coef, prior_rhs):
    n_times = lax.axis_size("tm")
    n_space, n_obs = lax.axis_size("space"), lax.axis_size("obs")
    n_cells = n_space * n_obs
    time_index = lax.axis_index("tm")
    nodes = obs_panel.shape[1]
    count = spatial_prec.shape[1]
    size = count + SPARE
    assert nodes % BLOCK == 0 and count % SPARE == 0
    cells = cell_table()
    first_row = cells[0] * count
    own_prec, coef = spatial_prec[0], ar_coef.reshape(1, 1)
    (own_pack,) = on_chip(
        pack_kernel,
        "pack_prior",
        [((size, nodes), jnp.bfloat16)],
        [],
        (cells, own_prec, coef, prior_rhs),
        0,
    )
    own_pack, route_time = lax.optimization_barrier((own_pack, route_time))
    from_next = shift(own_pack, "tm", -1)
    own_pieces = spread(own_pack)
    parts = routed_rows(obs_panel, node_index, weight, residual, route_time, n_times)
    next_pieces = spread(from_next)
    parts[1:], own_pieces[:n_space], next_pieces[:n_space] = lax.optimization_barrier(
        (parts[1:], own_pieces[:n_space], next_pieces[:n_space])
    )
    arrived = jnp.concatenate(parts, axis=1)
    near = [arrived] + [shift(arrived, "obs", e) for e in range(1, n_obs)]
    gram = sum(moments(part, nodes) for part in near)
    for d in range(1, n_space):
        slots = [shift(part, "space", d) for part in parts]
        slots[1:], gram = lax.optimization_barrier((slots[1:], gram))
        far = jnp.concatenate(slots, axis=1)
        gram = gram + moments(far, nodes)
        for e in range(1, n_obs):
            gram = gram + moments(shift(far, "obs", e), nodes)

    loss_right, loss_left, pack_fill, pack_turn, fill_one, diag_one, rhs_one = on_chip(
        functools.partial(first_kernel, n_cells),
        "level_one",
        [((size, nodes), jnp.bfloat16)] * 4
        + [
            ((count, nodes), jnp.float32),
            ((count, nodes), jnp.float32),
            ((8, nodes), jnp.float32),
        ],
        [
            ((nodes, nodes), jnp.float32),
            ((2 * count, nodes), jnp.float32),
            ((nodes, nodes), jnp.bfloat16),
            ((nodes, nodes), jnp.bfloat16),
        ]
        + solve_scratch(),
        (cells, coef, own_prec, gram, *own_pieces, *next_pieces),
        70 * nodes**3,
    )
    def is_second(time):
        return time % 4 == 2

    def after_one(time):
        return time % 4 == 1

    def before_none(time):
        return time % 4 == 3

    came_left = shift(loss_right, "tm", 1, after_one)
    came_right = shift(loss_left, "tm", -1, before_none)
    pack_fill, pack_turn, came_left, came_right = lax.optimization_barrier(
        (pack_fill, pack_turn, came_left, came_right)
    )
    fill_left = shift(pack_fill, "tm", 1, after_one)
    fill_right = shift(pack_turn, "tm", -1, before_none)

    pack_two, diag_two, rhs_two = on_chip(
        merge_kernel,
        "merge_losses",
        [
            ((size, nodes), jnp.bfloat16),
            ((count, nodes), jnp.float32),
            ((8, nodes), jnp.float32),
        ],
        [],
        (cells, diag_one, rhs_one, came_left, came_right),
        0,
    )
    pieces_two = spread(pack_two)
    fill_left, fill_right, pieces_two[0], loss_right, loss_left = lax.optimization_barrier(
        (fill_left, fill_right, pieces_two[0], loss_right, loss_left)
    )
    partner = jnp.concatenate([fill_left, fill_right], axis=0)
    partners = spread_at_once(partner)
    late_left = shift(loss_right, "tm", 1, before_none)
    late_right = shift(loss_left, "tm", -1, after_one)
    solved, rhs_full = on_chip(
        functools.partial(second_kernel, n_cells),
        "level_two",
        [((2 * count, nodes), jnp.float32), ((8, nodes), jnp.float32)],
        [((nodes, nodes), jnp.float32)] + solve_scratch(),
        (cells, partner, *pieces_two),
        60 * nodes**3,
    )
    together = 4 % n_times == 0
    loss_two, fill_two = on_chip(
        functools.partial(last_kernel, n_cells, together),
        "products_two",
        [
            ((size if together else 2 * size, nodes), jnp.bfloat16),
            ((count, nodes), jnp.float32),
        ],
        [((nodes, nodes), jnp.bfloat16), ((nodes, nodes), jnp.bfloat16)],
        (cells, solved, rhs_full, partner, *partners),
        4 * nodes**3,
    )

    if together:
        came = [shift(loss_two, "tm", 2, is_second)]
    else:
        came = [
            shift(loss_two[:size], "tm", -2, is_second),
            shift(loss_two[size:], "tm", 2, is_second),
        ]
    mask = diagonal_mask(count, nodes, first_row)
    diag_out = diag_two - unpack_rows(late_left, mask) - unpack_rows(late_right, mask)
    rhs_out = rhs_two[0] - unpack_vector(late_left) - unpack_vector(late_right)
    for part in came:
        diag_out = diag_out - unpack_rows(part, mask)
        rhs_out = rhs_out - unpack_vector(part)
    rhs_out = lax.dynamic_slice_in_dim(rhs_out, first_row, count, 0)
    fill_out = jnp.where(
        time_index % 2 == 1,
        fill_one,
        jnp.where(is_second(time_index), fill_two, jnp.zeros_like(fill_two)),
    )
    return (diag_out[None], fill_out[None], rhs_out[None])


def solution(mesh):
    return jax.shard_map(
        local,
        mesh=mesh,
        in_specs=(
            P(("grp", "tm", "space", "obs"), None),
            P(("grp", "tm", "space", "obs")),
            P(("grp", "tm", "space", "obs")),
            P(("grp", "tm", "space", "obs")),
            P(("grp", "tm", "space", "obs")),
            P(("grp", "tm"), ("space", "obs"), None),
            P(("grp", "tm")),
            P(("grp", "tm"), ("space", "obs")),
        ),
        out_specs=(
            P(("grp", "tm"), ("space", "obs"), None),
            P(("grp", "tm"), ("space", "obs"), None),
            P(("grp", "tm"), ("space", "obs")),
        ),
        check_vma=False,
    )
```
